256 devices in a mesh: gx: 16 (over y_lo, z), gy: 16 (over y_hi, x, core).
Axes of the slice: x: 4, y: 4 (y_hi: 2, y_lo: 2; y = y_hi * 2 + y_lo), z: 8, core: 2. Of those that a mesh axis runs over, the one named last changes fastest.
Arguments:
- populations: float32 [19, 16, 64, 4096], P(None, None, 'gx', 'gy'), may hold values from -6 to 6
- fraction: float32 [32, 3, 4096], P('gx', None, 'gy'), may hold values from 0 to 1
- spans: int32 [32, 32, 1], P('gx'), may hold values from 0 to 15; in each aligned block of 64 rows (0 to 63, 64 to 127, ..., all dimensions but the last counted through in order) at most 8 rows name the same one
- stiffness: int32 [32], P('gx'), may hold values from 1 to 8
Outputs:
- populations_out: float32 [19, 16, 64, 4096], P(None, None, 'gx', 'gy')
- marker_vel: float32 [32, 3, 4096], P('gx', None, 'gy')
The draws below stay inside these ranges and needn't reach their ends.
Inputs may be any that keep to these rules, and one draw needn't show every extreme that they name: `spans`: among the 64 blocks of the filaments of one gx index, no tile is named by more than 8 blocks, and one is named by exactly 8.
All inputs are finite; a program needn't handle non-finite values.
Results may differ from the reference program's by a relative error of at most 0.0003.
Values sent between devices are 32-bit elements; how exact they have to be, the bound alone decides.
A program may use at most 64 MiB of HBM per device.

```python
import math
import jax
import jax.numpy as jnp
import numpy as np

CX = 4
CY = 256
NZ = 16
STEPS = 2
FIL_ROW = 2
M = 4096
FIL = 32
NB = 32
BMAX = 8
NX = 64
NY = 4096
N_GY = 16


def plant(values, stream_key, low, high):
    spot = [jax.random.randint(jax.random.fold_in(stream_key, axis), (), 0, length) for axis, length in enumerate(values.shape)]
    widest = values.shape.index(max(values.shape))
    beside = spot[:widest] + [(spot[widest] + 1) % values.shape[widest]] + spot[widest + 1:]
    return values.at[tuple(spot)].set(low).at[tuple(beside)].set(high)


def levels(own_key, dims, pieces, least, top_value):
    factor_of = 1.0
    for axis_at, shards_of in pieces:
        draws = jax.random.uniform(jax.random.fold_in(jax.random.fold_in(own_key, 6), axis_at), (shards_of,), jnp.float32, least / len(pieces), top_value / len(pieces))
        factor_of = factor_of * jnp.repeat(jnp.exp(draws), dims[axis_at] // shards_of).reshape((-1,) + (1,) * (len(dims) - 1 - axis_at))
    return factor_of


def deal_out(key, own, number, rows, number_of, top, limit, slope):
    order = jax.random.permutation(key, number_of)
    heavy_load, usual = portions_of(number_of, rows * top, limit, slope, True), portions_of(number_of, rows * top, limit, slope, False)
    places = jnp.arange(number_of)

    def named(lengths, rotation):
        used = int((lengths > 0).sum())
        fixed = max(1, used // 4)
        shifted = fixed + (places - fixed + rotation * (used - fixed)) % max(1, number_of - fixed)
        return jnp.zeros((number_of,), jnp.int32).at[order[jnp.where(places < fixed, places, shifted)]].set(jnp.asarray(lengths, jnp.int32))

    lengths = jnp.where(number % 4 == 0, named(heavy_load, number // 4), named(usual, number - number // 4 - 1))
    mixed = jax.random.permutation(jax.random.fold_in(own, 3), number_of)
    source_of, receiver = mixed[0:number_of // 2 * 2:2], mixed[1:number_of // 2 * 2:2]
    slack = jnp.minimum(lengths[source_of] - 1, limit - lengths[receiver]) // 2
    slack = jnp.where((source_of == order[0]) | (receiver == order[0]) | (lengths[receiver] == 0), 0, jnp.maximum(slack, 0))
    shifted = jax.random.randint(jax.random.fold_in(own, 4), (number_of // 2,), 0, 1 << 20) % (slack + 1)
    lengths = lengths.at[source_of].add(-shifted).at[receiver].add(shifted)
    labels = jnp.searchsorted(jnp.cumsum(lengths), jnp.arange(rows * top), side="right").astype(jnp.int32)
    table = labels.reshape(top, rows).T
    table = table[jax.random.permutation(jax.random.fold_in(own, 1), rows)]
    rotation = jax.random.randint(jax.random.fold_in(own, 2), (rows, 1), 0, top)
    return jnp.take_along_axis(table, (jnp.arange(top)[None, :] + rotation) % top, axis=1)


def portions_of(amount, total, most, skew, full):
    weights = [(1 << 20) // math.isqrt(standing ** skew) + 1 for standing in range(1, amount + 1)]
    largest = most if full else min(most, max(-(-total // amount), total * weights[0] // sum(weights)))
    least = 1 if total - largest >= amount - 1 else 0
    holding, surplus = [largest] + [least] * (amount - 1), total - largest - least * (amount - 1)
    while surplus > 0:
        free = [i for i in range(1, amount) if holding[i] < largest] or [i for i in range(1, amount) if holding[i] < most]
        whole, remaining = sum([weights[i] for i in free]), surplus
        for i in free:
            extra = min(most - holding[i], max(1, remaining * weights[i] // whole), surplus)
            holding[i] = holding[i] + extra
            surplus = surplus - extra
    return np.array(holding)


def gaussian(own_key, extent, width, reach, split=(), kind=jnp.bfloat16):
    entries = width * jax.random.normal(own_key, extent, jnp.float32)
    if split:
        entries = entries * levels(own_key, extent, split, -0.22, 0.18)
    return jnp.clip(entries, -reach, reach).astype(kind)


def setup_inputs(seed: int = 0) -> dict:
    keys = jax.random.split(jax.random.key(seed), 5)
    populations = gaussian(keys[0], (19, NZ, NX, NY), 1.0, 6.0, ((2, 16), (3, 16)), jnp.float32)
    fraction = jnp.clip(1.0 * jax.random.uniform(keys[1], (FIL, 3, M), jnp.float32) ** levels(keys[1], (FIL, 3, M), ((0, 16), (2, 16)), -0.2, 0.2), 0.0, 1.0)
    spans_keys = jax.random.split(jax.random.fold_in(keys[2], 1), FIL * NB // (FIL_ROW * NB))
    spans_turns = jax.random.permutation(jax.random.fold_in(keys[2], 3), FIL * NB // (FIL_ROW * NB))
    spans = jax.vmap(lambda own, number: deal_out(jax.random.fold_in(keys[2], 2), own, number, FIL_ROW * NB, N_GY, 1, BMAX, 2))(spans_keys, spans_turns).reshape((FIL, NB, 1))
    stiffness = plant(jax.random.randint(keys[3], (FIL,), 1, 9), jax.random.fold_in(keys[3], 1), 1, 8).astype(jnp.int32)
    return dict(populations=populations, fraction=fraction, spans=spans, stiffness=stiffness)


velocity_set = ((0, 0, 0), (1, 0, 0), (-1, 0, 0), (0, 1, 0), (0, -1, 0), (0, 0, 1), (0, 0, -1),
                (1, 1, 0), (-1, -1, 0), (1, -1, 0), (-1, 1, 0), (1, 0, 1), (-1, 0, -1),
                (1, 0, -1), (-1, 0, 1), (0, 1, 1), (0, -1, -1), (0, 1, -1), (0, -1, 1))
lattice_weight = (1.0 / 3.0,) + (1.0 / 18.0,) * 6 + (1.0 / 36.0,) * 12
relax_time = 0.8
deviation_unit = 0.002
feedback_gain = 2.0
stiff_unit = 0.002


def opposite(entry):
    return entry + 1 if entry % 2 == 1 else entry - 1


def kernel_weight(distance):
    return jnp.where(jnp.abs(distance) < 2.0, 0.25 * (1.0 + jnp.cos((0.5 * math.pi) * distance)), 0.0)


def periodic_gap(gap, period):
    half = 0.5 * period
    return jnp.where(gap > half, gap - period, jnp.where(gap < -half, gap + period, gap))


def marker_places(fraction, spans, row_anchor, tile_x, tile_y, depth):
    block_size = fraction.shape[2] // spans.shape[1]
    span_cells = jnp.repeat(spans[:, :, 0] * tile_y, block_size, axis=1).astype(jnp.float32)
    xpos = row_anchor[:, None] + 1.0 + fraction[:, 0] * (tile_x - 3.01)
    ypos = span_cells + fraction[:, 1] * tile_y
    zpos = 1.0 + fraction[:, 2] * (depth - 3.01)
    return jnp.stack([xpos, ypos, zpos], axis=1)


def elastic(places, period):
    ahead = places[:, :, 1:] - places[:, :, :-1]
    ahead = jnp.stack([ahead[:, 0], periodic_gap(ahead[:, 1], period), ahead[:, 2]], axis=1)
    edge = jnp.zeros(ahead.shape[:2] + (1,), jnp.float32)
    return jnp.concatenate([ahead, edge], 2) - jnp.concatenate([edge, ahead], 2)


def project(vector, parts, like):
    total = jnp.zeros_like(like)
    for axis_dim in range(3):
        if vector[axis_dim] != 0:
            total = total + float(vector[axis_dim]) * parts[axis_dim]
    return total


def moments(deviation):
    fpop = [lattice_weight[entry] + deviation_unit * deviation[entry] for entry in range(19)]
    dens = fpop[0]
    for entry in range(1, 19):
        dens = dens + fpop[entry]
    momentum = []
    for axis_dim in range(3):
        total = jnp.zeros_like(dens)
        for entry in range(19):
            if velocity_set[entry][axis_dim] != 0:
                total = total + float(velocity_set[entry][axis_dim]) * fpop[entry]
        momentum.append(total)
    return fpop, dens, momentum


def relax(fpop, dens, momentum, force):
    velocity = [(momentum[axis_dim] + 0.5 * force[axis_dim]) / dens for axis_dim in range(3)]
    speed_sq = velocity[0] * velocity[0] + velocity[1] * velocity[1] + velocity[2] * velocity[2]
    factor = 1.0 - 0.5 / relax_time
    drift_base = -(velocity[0] * force[0] + velocity[1] * force[1] + velocity[2] * force[2])
    post = []
    for entry in range(19):
        vector = velocity_set[entry]
        along = project(vector, velocity, dens)
        push = project(vector, force, dens)
        drift = push + drift_base
        equil = lattice_weight[entry] * dens * (1.0 + 3.0 * along + 4.5 * along * along - 1.5 * speed_sq)
        source = factor * lattice_weight[entry] * (3.0 * drift + 9.0 * along * push)
        post.append(fpop[entry] - (fpop[entry] - equil) / relax_time + source)
    return post


def bounce(moved, post):
    result = []
    for entry in range(19):
        lift = velocity_set[entry][2]
        plane = moved[entry]
        if lift == 1:
            plane = jnp.concatenate([post[opposite(entry)][:1], plane[:-1]], 0)
        elif lift == -1:
            plane = jnp.concatenate([plane[1:], post[opposite(entry)][-1:]], 0)
        result.append((plane - lattice_weight[entry]) / deviation_unit)
    return jnp.stack(result)


def stencil_parts(places):
    base = jnp.floor(places).astype(jnp.int32)
    cells = base[..., None] + jnp.arange(-1, 3, dtype=jnp.int32)
    weights = kernel_weight(places[..., None] - cells.astype(jnp.float32))
    zcell = cells[:, 2][:, :, :, None, None]
    xcell = cells[:, 0][:, :, None, :, None]
    ycell = jnp.mod(cells[:, 1], NY)[:, :, None, None, :]
    joint = weights[:, 2][:, :, :, None, None] * weights[:, 0][:, :, None, :, None]
    joint = joint * weights[:, 1][:, :, None, None, :]
    shape = joint.shape
    return (jnp.broadcast_to(zcell, shape), jnp.broadcast_to(xcell, shape), jnp.broadcast_to(ycell, shape), joint)


def interpolate(flow, parts):
    zcell, xcell, ycell, joint = parts
    values = [jnp.sum(flow[axis_dim][zcell, xcell, ycell] * joint, axis=(2, 3, 4)) for axis_dim in range(3)]
    return jnp.stack(values, axis=1)


def spread(force, parts):
    zcell, xcell, ycell, joint = parts
    fields = []
    for axis_dim in range(3):
        grid = jnp.zeros((NZ, NX, NY), jnp.float32)
        fields.append(grid.at[zcell, xcell, ycell].add(force[:, axis_dim][:, :, None, None, None] * joint))
    return fields


def reference(populations, fraction, spans, stiffness):
    row_anchor = ((jnp.arange(FIL, dtype=jnp.int32) // FIL_ROW) * CX).astype(jnp.float32)
    places = marker_places(fraction, spans, row_anchor, CX, CY, NZ)
    parts = stencil_parts(places)
    bend = elastic(places, NY) * (stiffness.astype(jnp.float32) * (stiff_unit / CY))[:, None, None]
    deviation = populations
    marker_speed = jnp.zeros((FIL, 3, M), jnp.float32)
    for step in range(STEPS):
        fpop, dens, momentum = moments(deviation)
        flow = jnp.stack([part / dens for part in momentum])
        marker_speed = interpolate(flow, parts)
        force = bend - feedback_gain * marker_speed
        field_force = spread(force, parts)
        post = relax(fpop, dens, momentum, field_force)
        moved = []
        for entry in range(19):
            shift_x, shift_y = velocity_set[entry][0], velocity_set[entry][1]
            moved.append(jnp.roll(post[entry], (shift_x, shift_y), axis=(1, 2)))
        deviation = bounce(moved, post)
    return deviation, marker_speed / deviation_unit
```

```python
import functools
import math

import jax
import jax.numpy as jnp
from jax import lax
from jax.experimental import pallas as pl
from jax.experimental.pallas import tpu as pltpu
from jax.sharding import PartitionSpec as P

F32 = jnp.float32
BF16 = jnp.bfloat16
MESH = pl.DeviceIdType.MESH

velocity_set = (
    (0, 0, 0), (1, 0, 0), (-1, 0, 0), (0, 1, 0), (0, -1, 0), (0, 0, 1), (0, 0, -1),
    (1, 1, 0), (-1, -1, 0), (1, -1, 0), (-1, 1, 0), (1, 0, 1), (-1, 0, -1),
    (1, 0, -1), (-1, 0, 1), (0, 1, 1), (0, -1, -1), (0, 1, -1), (0, -1, 1),
)
lattice_weight = (1.0 / 3.0,) + (1.0 / 18.0,) * 6 + (1.0 / 36.0,) * 12
relax_time = 0.8
deviation_unit = 0.002
feedback_gain = 2.0
stiff_unit = 0.002

STRIP = (9, 1, 11, 13, 7, 3, 15, 17, 10, 2, 12, 14, 8, 4, 16, 18, 9, 0, 5, 6)
AT = {entry: STRIP.index(entry) for entry in range(19)}
EAST, WEST = STRIP[0:5], STRIP[8:13]
PAIRS = tuple((i, i + 1) for i in range(1, 19, 2))


def opposite(entry):
    return entry + 1 if entry % 2 == 1 else entry - 1


def moments(f):
    rho = f[0]
    for entry in range(1, 19):
        rho = rho + f[entry]
    flux = []
    for dim in range(3):
        total = None
        for a, b in PAIRS:
            c = velocity_set[a][dim]
            if c:
                term = f[a] - f[b] if c > 0 else f[b] - f[a]
                total = term if total is None else total + term
        flux.append(total)
    return rho, flux


def project(vector, parts):
    total = None
    for dim in range(3):
        if vector[dim]:
            if total is None:
                total = parts[dim] if vector[dim] > 0 else -parts[dim]
            else:
                total = total + parts[dim] if vector[dim] > 0 else total - parts[dim]
    return total


def collide(f, rho, flux, force):
    factor = 1.0 - 0.5 / relax_time
    keep, gain = 1.0 - 1.0 / relax_time, 1.0 / relax_time
    mom = [flux[d] + 0.5 * force[d] for d in range(3)]
    inv = 1.0 / rho
    u = [mom[d] * inv for d in range(3)]
    usq = u[0] * mom[0] + u[1] * mom[1] + u[2] * mom[2]
    ug = u[0] * force[0] + u[1] * force[1] + u[2] * force[2]
    base = gain * (rho - 1.5 * usq) - (3.0 * factor) * ug
    post = [None] * 19
    post[0] = keep * f[0] + lattice_weight[0] * base
    for a, b in PAIRS:
        vector = velocity_set[a]
        cu, cm, cg = project(vector, u), project(vector, mom), project(vector, force)
        even = base + cu * ((4.5 * gain) * cm + (9.0 * factor) * cg)
        odd = (3.0 * gain) * cm + (3.0 * factor) * cg
        w = lattice_weight[a]
        post[a] = keep * f[a] + w * (even + odd)
        post[b] = keep * f[b] + w * (even - odd)
    return post


def split(a):
    hi = a.astype(BF16)
    return hi, (a - hi.astype(F32)).astype(BF16)


def dot3(a, bh, bl):
    ah, al = split(a)
    d = functools.partial(jnp.dot, preferred_element_type=F32)
    return d(ah, bh) + (d(ah, bl) + d(al, bh))


def dot3t(a, bh, bl):
    ah, al = split(a)
    d = lambda x, y: lax.dot_general(x, y, (((1,), (1,)), ((), ())), preferred_element_type=F32)
    return d(ah, bh) + (d(ah, bl) + d(al, bh))


def dot_select(pick, b):
    h = b.astype(BF16)
    rest = b - h.astype(F32)
    m = rest.astype(BF16)
    l = (rest - m.astype(F32)).astype(BF16)
    d = functools.partial(jnp.dot, preferred_element_type=F32)
    return (d(pick, h) + d(pick, m)) + d(pick, l)


def pattern(n):
    m = n & 3
    one, zero = jnp.float32(1.0), jnp.float32(0.0)
    c = jnp.where(m == 0, one, jnp.where(m == 2, -one, zero))
    s = jnp.where(m == 1, one, jnp.where(m == 3, -one, zero))
    return n.astype(F32), c, s


def weight(row, pat):
    x, c, s = row
    n, cp, sp = pat
    return jnp.where(jnp.abs(x - n) < 2.0, 0.25 + 0.25 * (c * cp + s * sp), 0.0)


def iota(shape, dim):
    return lax.broadcasted_iota(jnp.int32, shape, dim)


def kernel(nx, ny, pop, frac, spans, stiff, out_pop, out_vel,
           fm, mo, fl, lf, gf, pm, fr_send, fr_all, data, sel_t, xyz, bend, wm_h, wm_l, plane,
           ws_h, ws_l, wx, brow, urow, us, u_ret, u_recv,
           p_flow, fl_l, fl_r, sf, st, p1, r1l, r1r, gxa, gxb, daa, dab, dba, dbb,
           p2, r2l, r2r, d2aa, d2ab, d2ba, d2bb, xsp, xsm, xrp, xrm, gs,
           ag_s, ag_r, u_s, u_r, k_s, k_r):
    me_x, me_y = lax.axis_index("gx"), lax.axis_index("gy")
    east, west = lax.rem(me_x + 1, nx), lax.rem(me_x + nx - 1, nx)
    north, south = lax.rem(me_y + 1, ny), lax.rem(me_y + ny - 1, ny)
    tile_y = 256

    barrier = pltpu.get_barrier_semaphore()
    partners = [(me_x, lax.rem(me_y + d, ny)) for d in range(1, ny)]
    partners += [(east, me_y), (west, me_y), (east, north), (east, south), (west, north), (west, south)]
    for partner in partners:
        pl.semaphore_signal(barrier, inc=1, device_id=partner, device_id_type=MESH)

    def remote(src, dst, k, target):
        copy = pltpu.make_async_remote_copy(
            src_ref=src, dst_ref=dst, send_sem=k_s.at[k], recv_sem=k_r.at[k],
            device_id=target, device_id_type=MESH)
        copy.start()
        return copy

    lane, sub = iota((8, 128), 1), iota((8, 128), 0)
    cell, zl, xs = lane & 7, lane >> 3, sub & 3
    own = (sub >> 2) + (cell >> 2) == 1
    edge1 = ((sub < 4) & (lane == 0), (sub >= 4) & (lane == 127))
    edge4 = (lane >> 2) + (sub >> 2) * 32 == 0
    edge4 = edge4 | ((sub >= 4) & (lane >= 124))

    def first(z, carry):
        f = []
        for entry in range(19):
            f.append(lattice_weight[entry] + deviation_unit * pop[entry, z])
            fm[entry, z] = f[entry]
        rho, flux = moments(f)
        mo[0, z] = rho
        inv = 1.0 / rho
        for d in range(3):
            mo[1 + d, z] = flux[d]
            fl[d, z] = flux[d] * inv
        return carry

    lax.fori_loop(0, 16, first, 0)

    def pack(ref, n):
        def body(z, acc):
            rolled = pltpu.roll(ref[:, z], 8 * z + 4, 2)
            return jnp.where(zl[None] == z, rolled, acc)
        return lax.fori_loop(0, 16, body, jnp.zeros((n, 8, 128), F32))

    p_flow[...] = pack(fl, 3)
    for c in range(3):
        for f in range(2):
            fr_send[2 * c + f : 2 * c + f + 1, :] = frac[c, f : f + 1, :]
    fr_send[6:8, :] = jnp.zeros((2, 256), F32)
    fr_all[me_y] = fr_send[...]

    pl.semaphore_wait(barrier, len(partners))
    gathers = []
    for d in range(1, ny):
        copy = pltpu.make_async_remote_copy(
            src_ref=fr_send, dst_ref=fr_all.at[me_y], send_sem=ag_s.at[d], recv_sem=ag_r.at[d],
            device_id=(me_x, lax.rem(me_y + d, ny)), device_id_type=MESH)
        copy.start()
        gathers.append(copy)
    flows = [remote(p_flow, fl_l, 0, (me_x, north)), remote(p_flow, fl_r, 1, (me_x, south))]

    st[...] = pack(fm, 19)

    def rows_of_flow():
        v = fl[...].reshape(3, 8, 2, 8, 128)
        a, b = v[:, :, 0].reshape(24, 8, 128), v[:, :, 1].reshape(24, 8, 128)
        low = (sub < 4)[None]
        lf[:, 0:128] = jnp.where(low, a, pltpu.roll(b, 4, 1)).reshape(192, 128)
        lf[:, 128:256] = jnp.where(low, pltpu.roll(a, 4, 1), b).reshape(192, 128)

    rows_of_flow()

    span_cols = []
    row16, lane32 = iota((16, 32), 0), iota((16, 32), 1)
    for f in range(2):
        line = jnp.broadcast_to(spans[f : f + 1, :].astype(F32), (16, 32))
        for i in range(2):
            span_cols.append(jnp.sum(jnp.where(lane32 == 2 * row16 + i, line, 0.0), axis=1, keepdims=True))
    span_col = jnp.concatenate(span_cols + [jnp.full((64, 1), -1.0, F32)], axis=0)
    r128, l128 = iota((128, 128), 0), iota((128, 128), 1)
    target = me_y + (l128 >> 3) - 1
    target = jnp.where(target < 0, target + ny, jnp.where(target >= ny, target - ny, target)).astype(F32)
    match = jnp.where((jnp.broadcast_to(span_col, (128, 128)) == target) & (l128 < 24), 1.0, 0.0)
    before = jnp.where(l128 < r128, 1.0, 0.0).astype(BF16)
    rank = jnp.dot(before, match.astype(BF16), preferred_element_type=F32)
    chosen = jnp.where(rank == (l128 & 7).astype(F32), match, 0.0)
    sel_t[...] = chosen
    sel = chosen.T
    valid = jnp.sum(sel, axis=1, keepdims=True)[0:32]
    pick = sel[0:32].astype(BF16)

    for copy in gathers:
        copy.wait()
    anchor = (me_x * 4).astype(F32)
    l16, r16 = iota((16, 128), 1), iota((16, 128), 0)
    zero64 = jnp.zeros((64, 128), F32)
    for q in range(6):
        data[q, 64:128] = zero64
    for f in range(2):
        strength = stiff[f].astype(F32) * (stiff_unit / tile_y)
        for c in range(3):
            x = []
            for i in range(2):
                part = fr_all[:, 2 * c + f, i * 128 : (i + 1) * 128]
                if c == 0:
                    x.append((anchor + 1.0) + part * (4 - 3.01))
                elif c == 1:
                    x.append(span_cols[2 * f + i] * tile_y + part * tile_y)
                else:
                    x.append(1.0 + part * (16 - 3.01))
            ahead = [pltpu.roll(x[i], 127, 1) for i in range(2)]
            g0 = jnp.where(l16 == 127, ahead[1], ahead[0]) - x[0]
            g1 = jnp.where(l16 == 127, pltpu.roll(ahead[0], 15, 0), ahead[1]) - x[1]
            if c == 1:
                period = float(ny * tile_y)
                half = 0.5 * period
                g0 = jnp.where(g0 > half, g0 - period, jnp.where(g0 < -half, g0 + period, g0))
                g1 = jnp.where(g1 > half, g1 - period, jnp.where(g1 < -half, g1 + period, g1))
            g1 = jnp.where((l16 == 127) & (r16 == 15), 0.0, g1)
            b0, b1 = pltpu.roll(g0, 1, 1), pltpu.roll(g1, 1, 1)
            prev0 = jnp.where(l16 == 0, pltpu.roll(b1, 1, 0), b0)
            prev1 = jnp.where(l16 == 0, b0, b1)
            at = f * 32
            data[c, at : at + 16] = x[0]
            data[c, at + 16 : at + 32] = x[1]
            data[3 + c, at : at + 16] = (g0 - prev0) * strength
            data[3 + c, at + 16 : at + 32] = (g1 - prev1) * strength
    for c in range(3):
        bend[c] = dot_select(pick, data[3 + c])
        x = dot_select(pick, data[c])
        if c == 0:
            x = x - anchor
        elif c == 1:
            x = x - (me_y * tile_y).astype(F32)
            period = float(ny * tile_y)
            x = jnp.where(x > 0.5 * period, x - period, jnp.where(x < -0.5 * period, x + period, x))
            x = jnp.where(valid > 0.5, x, 1.0e6)
        base = jnp.floor(x)
        part = (0.5 * math.pi) * (x - base)
        cos, sin = jnp.cos(part), jnp.sin(part)
        turn = base - 4.0 * jnp.floor(0.25 * base)
        xyz[c, 0] = x
        xyz[c, 1] = jnp.where(turn == 0.0, cos, jnp.where(turn == 1.0, -sin, jnp.where(turn == 2.0, -cos, sin)))
        xyz[c, 2] = jnp.where(turn == 0.0, sin, jnp.where(turn == 1.0, cos, jnp.where(turn == 2.0, -sin, -cos)))

    pat_y = pattern(iota((256, 128), 0))
    r64 = iota((64, 128), 0)
    pat_pz, pat_px = pattern(r64 >> 2), pattern(r64 & 3)
    pat_sz = pattern(r128 >> 3)
    pat_low, pat_high = pattern((r128 & 7) - 4), pattern((r128 & 7) + (tile_y - 4))
    pat_x = pattern(xs)

    def weights(s, carry):
        def line(group, c):
            return [xyz[c, k, pl.ds(group * 8 + s, 1), :] for k in range(3)]
        where_s = pl.ds(pl.multiple_of(s * 128, 128), 128)

        def put_strip(slot, value):
            columns = pl.ds(pl.multiple_of(slot * 1024 + s * 128, 128), 128)
            hi, lo = split(value)
            ws_h[:, columns] = hi
            ws_l[:, columns] = lo

        for group in range(3):
            lx, ly, lz = line(group, 0), line(group, 1), line(group, 2)
            wx[group, :, where_s] = weight(lx, pat_x)
            wz = weight(lz, pat_sz)
            if group < 2:
                put_strip(0 if group == 0 else 2, wz * weight(ly, pat_low))
            if group > 0:
                put_strip(1 if group == 2 else 3, wz * weight(ly, pat_high))
            if group == 1:
                hi, lo = split(weight(ly, pat_y))
                wm_h[:, where_s] = hi
                wm_l[:, where_s] = lo
                plane[:, where_s] = weight(lz, pat_pz) * weight(lx, pat_px)
            for c in range(3):
                brow[group, c : c + 1, where_s] = bend[c, pl.ds(group * 8 + s, 1), :]
        return carry

    lax.fori_loop(0, 8, weights, 0)
    for group in range(3):
        brow[group, 3:8, :] = jnp.zeros((5, 1024), F32)

    def merge(centre, left, right):
        n = centre.shape[0]
        side = jnp.where((cell < 4)[None], left, right)
        return jnp.where(own[None], centre, pltpu.roll(side, 4, 1))

    left_side = jnp.where(iota((8, 1024), 0) < 4, 1.0, 0.0)
    right_side = 1.0 - left_side

    def interpolate_spread():
        full = jnp.concatenate([sf[0], sf[1], sf[2], jnp.zeros((8, 128), F32)], axis=0)
        halo = jnp.concatenate([jnp.where(own, 0.0, sf[d]) for d in range(3)] + [jnp.zeros((8, 128), F32)], axis=0)
        near = dot3(full, ws_h[:, 0:2048], ws_l[:, 0:2048])
        mine = dot3(halo, ws_h[:, 2048:4096], ws_l[:, 2048:4096])
        for c in range(3):
            a = near[8 * c : 8 * c + 8]
            b = mine[8 * c : 8 * c + 8]
            urow[0, c : c + 1, :] = jnp.sum(a[:, 0:1024] * (wx[0] * left_side), axis=0, keepdims=True)
            urow[2, c : c + 1, :] = jnp.sum(a[:, 1024:2048] * (wx[2] * right_side), axis=0, keepdims=True)
            both = b[:, 0:1024] * left_side + b[:, 1024:2048] * right_side
            urow[1, c : c + 1, :] = jnp.sum(both * wx[1], axis=0, keepdims=True)
        lh, ll = split(lf[...])
        d = functools.partial(jnp.dot, preferred_element_type=F32)
        for q in range(4):
            cols = slice(256 * q, 256 * q + 256)
            a = d(lh, wm_h[:, cols]) + (d(lh, wm_l[:, cols]) + d(ll, wm_h[:, cols]))
            for c in range(3):
                part = jnp.sum(a[64 * c : 64 * c + 64] * plane[:, cols], axis=0, keepdims=True)
                urow[1, c : c + 1, cols] = urow[1, c : c + 1, cols] + part

    def forces():
        return [brow[group] - feedback_gain * urow[group] for group in range(3)]

    def spread_strips(force):
        total = None
        for slot, (group, side) in enumerate(((0, left_side), (2, right_side), (1, left_side), (1, right_side))):
            w = wx[group] * side
            v = jnp.concatenate([force[group][c : c + 1] * w for c in range(3)] + [jnp.zeros((8, 1024), F32)], axis=0)
            cols = slice(1024 * slot, 1024 * slot + 1024)
            part = dot3t(v, ws_h[:, cols], ws_l[:, cols])
            total = part if total is None else total + part
        return [total[8 * c : 8 * c + 8] for c in range(3)]

    def spread_tile(force):
        total = None
        for q in range(4):
            cols = slice(256 * q, 256 * q + 256)
            v = jnp.concatenate([force[1][c : c + 1, cols] * plane[:, cols] for c in range(3)], axis=0)
            part = dot3t(v, wm_h[:, cols], wm_l[:, cols])
            total = part if total is None else total + part
        a, b = total[:, 0:128].reshape(24, 8, 128), total[:, 128:256].reshape(24, 8, 128)
        low = (sub < 4)[None]
        even = jnp.where(low, a, pltpu.roll(b, 4, 1)).reshape(24, 1, 8, 128)
        odd = jnp.where(low, pltpu.roll(a, 4, 1), b).reshape(24, 1, 8, 128)
        gf[...] = jnp.concatenate([even, odd], axis=1).reshape(3, 16, 8, 128)

    def collide_tile():
        def body(z, carry):
            f = [fm[entry, z] for entry in range(19)]
            force = []
            for d in range(3):
                force.append(jnp.where(edge4, pltpu.roll(gs[d], 124 - 8 * z, 1), gf[d, z]))
            post = collide(f, mo[0, z], [mo[1, z], mo[2, z], mo[3, z]], force)
            for entry in range(19):
                pm[entry, z] = post[entry]
            return carry
        lax.fori_loop(0, 16, body, 0)

    def pack_rows(send, entries, shift):
        for k, entry in enumerate(entries):
            v = pm[entry].reshape(4, 4, 8, 128)
            acc = pltpu.roll(v[:, 0], shift, 1) if shift else v[:, 0]
            for zz in range(1, 4):
                acc = jnp.where((xs == zz)[None], pltpu.roll(v[:, zz], (shift + zz) % 8, 1), acc)
            send[k] = acc

    def stream_strips(strip, ext_east, ext_west):
        result = {}
        for entry in strip["want"]:
            cx, cy, cz = velocity_set[entry]
            v = strip[entry]
            if cx == 1:
                v = jnp.where(xs == 0, ext_east[entry], pltpu.roll(v, 1, 0))
            elif cx == -1:
                v = jnp.where(xs == 3, ext_west[entry], pltpu.roll(v, 7, 0))
            turn = (8 * cz + cy) % 128
            if turn:
                v = pltpu.roll(v, turn, 1)
            if cz == 1:
                v = jnp.where(zl == 0, strip[opposite(entry)], v)
            elif cz == -1:
                v = jnp.where(zl == 15, strip[opposite(entry)], v)
            result[entry] = v
        return result

    def stream_at(entry, z, step):
        cx, cy, cz = velocity_set[entry]
        zs = jnp.maximum(z - 1, 0) if cz == 1 else jnp.minimum(z + 1, 15) if cz == -1 else z
        v = pm[entry, zs]
        if cx:
            zz = zs & 3
            if cx == 1:
                row = pltpu.roll(xrp[step, EAST.index(entry), zs >> 2], (8 - zz) & 7, 0)
                v = jnp.where(xs == 0, row, pltpu.roll(v, 1, 0))
            else:
                row = pltpu.roll(xrm[step, WEST.index(entry), zs >> 2], 3 - zz, 0)
                v = jnp.where(xs == 3, row, pltpu.roll(v, 7, 0))
        if cy:
            r = pltpu.roll(v, 1 if cy == 1 else 127, 1)
            v = jnp.where(lane == (0 if cy == 1 else 127), pltpu.roll(r, 4, 0), r)
        if cz:
            v = jnp.where(z == (0 if cz == 1 else 15), pm[opposite(entry), z], v)
        if cy:
            strip = pltpu.roll(st[entry], 124 - 8 * z, 1)
            v = jnp.where(edge1[0] if cy == 1 else edge1[1], strip, v)
        return v

    for copy in flows:
        copy.wait()
    sf[...] = merge(p_flow[...], fl_l[...], fl_r[...])
    interpolate_spread()
    force = forces()
    strip_force = spread_strips(force)
    for d in range(3):
        gs[d] = strip_force[d]
    f = [st[entry] for entry in range(19)]
    rho, flux = moments(f)
    post = collide(f, rho, flux, strip_force)
    for k, entry in enumerate(STRIP):
        p1[k] = post[entry]
    strips = [
        remote(p1, r1l, 2, (me_x, north)),
        remote(p1, r1r, 3, (me_x, south)),
        remote(p1.at[0:5], gxa, 4, (east, me_y)),
        remote(p1.at[8:13], gxb, 5, (west, me_y)),
        remote(p1.at[0:5], daa, 6, (east, north)),
        remote(p1.at[0:5], dab, 7, (east, south)),
        remote(p1.at[8:13], dba, 8, (west, north)),
        remote(p1.at[8:13], dbb, 9, (west, south)),
    ]
    spread_tile(force)
    collide_tile()
    pack_rows(xsp.at[0], EAST, 5)
    pack_rows(xsm.at[0], WEST, 0)
    rows = [remote(xsp.at[0], xrp.at[0], 10, (east, me_y)), remote(xsm.at[0], xrm.at[0], 11, (west, me_y))]

    for copy in strips:
        copy.wait()
    whole = merge(p1[...], r1l[...], r1r[...])
    beside_w = pltpu.roll(merge(gxa[...], daa[...], dab[...]), 5, 1)
    beside_e = pltpu.roll(merge(gxb[...], dba[...], dbb[...]), 3, 1)
    strip = {entry: whole[AT[entry]] for entry in range(19)}
    strip["want"] = range(19)
    moved = stream_strips(strip, {e: beside_w[k] for k, e in enumerate(EAST)},
                          {e: beside_e[k] for k, e in enumerate(WEST)})
    for entry in range(19):
        st[entry] = moved[entry]
    f = [moved[entry] for entry in range(19)]
    strip_rho, strip_flux = moments(f)
    inv = 1.0 / strip_rho
    for d in range(3):
        sf[d] = strip_flux[d] * inv
    for copy in rows:
        copy.wait()

    def second(z, carry):
        f = []
        for entry in range(19):
            v = stream_at(entry, z, 0)
            f.append(v)
            fm[entry, z] = v
        rho, flux = moments(f)
        mo[0, z] = rho
        inv = 1.0 / rho
        for d in range(3):
            mo[1 + d, z] = flux[d]
            fl[d, z] = flux[d] * inv
        return carry

    lax.fori_loop(0, 16, second, 0)
    rows_of_flow()

    interpolate_spread()
    force = forces()
    strip_force = spread_strips(force)
    for d in range(3):
        gs[d] = strip_force[d]
    f = [st[entry] for entry in range(19)]
    post = collide(f, strip_rho, strip_flux, strip_force)
    for k, entry in enumerate(STRIP):
        p2[k] = post[entry]
    strips = [
        remote(p2.at[4:9], r2l, 12, (me_x, north)),
        remote(p2.at[12:17], r2r, 13, (me_x, south)),
        remote(p2.at[4:5], d2aa, 14, (east, north)),
        remote(p2.at[0:1], d2ab, 15, (east, south)),
        remote(p2.at[8:9], d2ba, 16, (west, north)),
        remote(p2.at[12:13], d2bb, 17, (west, south)),
    ]
    spread_tile(force)
    collide_tile()
    pack_rows(xsp.at[1], EAST, 5)
    pack_rows(xsm.at[1], WEST, 0)
    rows = [remote(xsp.at[1], xrp.at[1], 18, (east, me_y)), remote(xsm.at[1], xrm.at[1], 19, (west, me_y))]

    for c in range(3):
        us[c] = jnp.zeros((128, 128), F32)
    def slots(s, carry):
        for c in range(3):
            us[c, pl.ds(8 + s, 1), :] = urow[1, c : c + 1, pl.ds(pl.multiple_of(s * 128, 128), 128)]
        return carry
    lax.fori_loop(0, 8, slots, 0)
    home = sel_t[0:64].astype(BF16)
    u_ret[...] = jnp.zeros((ny, 8, 256), F32)
    for c in range(3):
        back = dot_select(home, us[c])
        for f in range(2):
            for i in range(2):
                at = (2 * f + i) * 16
                u_ret[:, 2 * c + f, i * 128 : (i + 1) * 128] = back[at : at + 16]
    u_recv[me_y] = u_ret[me_y]
    returns = []
    for d in range(1, ny):
        peer = lax.rem(me_y + d, ny)
        copy = pltpu.make_async_remote_copy(
            src_ref=u_ret.at[peer], dst_ref=u_recv.at[me_y], send_sem=u_s.at[d], recv_sem=u_r.at[d],
            device_id=(me_x, peer), device_id_type=MESH)
        copy.start()
        returns.append(copy)

    for copy in strips:
        copy.wait()
    own_strip = {entry: p2[AT[entry]] for entry in range(19)}
    for k, entry in enumerate(STRIP[4:9]):
        own_strip[entry] = jnp.where(own, p2[AT[entry]], pltpu.roll(r2l[k], 4, 0))
    south_side = dict(own_strip)
    for k, entry in enumerate(STRIP[12:17]):
        south_side[entry] = jnp.where(own, p2[AT[entry]], pltpu.roll(r2r[k], 4, 0))
    south_side["want"] = STRIP[4:9] + STRIP[12:17]
    for k, entry in enumerate(STRIP[4:9]):
        south_side[entry] = own_strip[entry]
    moved = stream_strips(
        south_side,
        {7: pltpu.roll(d2aa[0], 1, 0), 9: pltpu.roll(d2ab[0], 1, 0)},
        {10: pltpu.roll(d2ba[0], 7, 0), 8: pltpu.roll(d2bb[0], 7, 0)})
    for entry in south_side["want"]:
        st[entry] = moved[entry]
    for copy in rows:
        copy.wait()

    def last(z, carry):
        for entry in range(19):
            v = stream_at(entry, z, 1)
            out_pop[entry, z] = (v - lattice_weight[entry]) * (1.0 / deviation_unit)
        return carry

    lax.fori_loop(0, 16, last, 0)

    for copy in returns:
        copy.wait()
    total = u_recv[0]
    for j in range(1, ny):
        total = total + u_recv[j]
    total = total / deviation_unit
    for c in range(3):
        for f in range(2):
            out_vel[c, f : f + 1, :] = total[2 * c + f : 2 * c + f + 1, :]


def per_device(nx, ny, populations, fraction, spans, stiffness):
    pop = populations.reshape(19, 16, 4, 2, 128).transpose(0, 1, 3, 2, 4).reshape(19, 16, 8, 128)
    vmem = pl.BlockSpec(memory_space=pltpu.VMEM)
    smem = pl.BlockSpec(memory_space=pltpu.SMEM)
    V = lambda *shape: pltpu.VMEM(shape, F32)
    B = lambda *shape: pltpu.VMEM(shape, BF16)
    dma = pltpu.SemaphoreType.DMA
    tile = V(19, 16, 8, 128)
    scratch = [
        tile, V(4, 16, 8, 128), V(3, 16, 8, 128), V(192, 256), V(3, 16, 8, 128), tile,
        V(8, 256), V(ny, 8, 256), V(6, 128, 128), V(128, 128), V(3, 3, 32, 128), V(3, 32, 128),
        B(256, 1024), B(256, 1024), V(64, 1024), B(128, 4096), B(128, 4096), V(3, 8, 1024),
        V(3, 8, 1024), V(3, 8, 1024), V(3, 128, 128), V(ny, 8, 256), V(ny, 8, 256),
        V(3, 8, 128), V(3, 8, 128), V(3, 8, 128), V(3, 8, 128), V(19, 8, 128),
        V(20, 8, 128), V(20, 8, 128), V(20, 8, 128),
        V(5, 8, 128), V(5, 8, 128), V(5, 8, 128), V(5, 8, 128), V(5, 8, 128), V(5, 8, 128),
        V(20, 8, 128), V(5, 8, 128), V(5, 8, 128), V(1, 8, 128), V(1, 8, 128), V(1, 8, 128), V(1, 8, 128),
        V(2, 5, 4, 8, 128), V(2, 5, 4, 8, 128), V(2, 5, 4, 8, 128), V(2, 5, 4, 8, 128), V(3, 8, 128),
        dma((ny,)), dma((ny,)), dma((ny,)), dma((ny,)), dma((20,)), dma((20,)),
    ]
    out, vel = pl.pallas_call(
        functools.partial(kernel, nx, ny),
        out_shape=(jax.ShapeDtypeStruct((19, 16, 8, 128), F32), jax.ShapeDtypeStruct((3, 2, 256), F32)),
        in_specs=[vmem, vmem, vmem, smem],
        out_specs=(vmem, vmem),
        scratch_shapes=scratch,
        name="lattice",
        compiler_params=pltpu.CompilerParams(
            collective_id=0, has_side_effects=True, vmem_limit_bytes=48 << 20),
    )(pop, fraction.transpose(1, 0, 2), spans.reshape(spans.shape[0], spans.shape[1]), stiffness)
    out = out.reshape(19, 16, 2, 4, 128).transpose(0, 1, 3, 2, 4).reshape(19, 16, 4, 256)
    return out, vel.transpose(1, 0, 2)


def solution(mesh):
    placed = (P(None, None, "gx", "gy"), P("gx", None, "gy"), P("gx", None, None), P("gx"))
    return jax.shard_map(
        functools.partial(per_device, mesh.shape["gx"], mesh.shape["gy"]),
        mesh=mesh,
        in_specs=placed,
        out_specs=(P(None, None, "gx", "gy"), P("gx", None, "gy")),
        check_vma=False,
    )
```

```python
import functools
import math

import jax
import jax.numpy as jnp
from jax import lax
from jax.experimental import pallas as pl
from jax.experimental.pallas import tpu as pltpu
from jax.sharding import PartitionSpec as P

F32 = jnp.float32
BF16 = jnp.bfloat16
MESH = pl.DeviceIdType.MESH

velocity_set = (
    (0, 0, 0), (1, 0, 0), (-1, 0, 0), (0, 1, 0), (0, -1, 0), (0, 0, 1), (0, 0, -1),
    (1, 1, 0), (-1, -1, 0), (1, -1, 0), (-1, 1, 0), (1, 0, 1), (-1, 0, -1),
    (1, 0, -1), (-1, 0, 1), (0, 1, 1), (0, -1, -1), (0, 1, -1), (0, -1, 1),
)
lattice_weight = (1.0 / 3.0,) + (1.0 / 18.0,) * 6 + (1.0 / 36.0,) * 12
relax_time = 0.8
deviation_unit = 0.002
feedback_gain = 2.0
stiff_unit = 0.002

STRIP = (9, 1, 11, 13, 7, 3, 15, 17, 10, 2, 12, 14, 8, 4, 16, 18, 9, 0, 5, 6)
AT = {entry: STRIP.index(entry) for entry in range(19)}
EAST, WEST = STRIP[0:5], STRIP[8:13]
PAIRS = tuple((i, i + 1) for i in range(1, 19, 2))


def opposite(entry):
    return entry + 1 if entry % 2 == 1 else entry - 1


def moments(f):
    rho = f[0]
    for entry in range(1, 19):
        rho = rho + f[entry]
    flux = []
    for dim in range(3):
        total = None
        for a, b in PAIRS:
            c = velocity_set[a][dim]
            if c:
                term = f[a] - f[b] if c > 0 else f[b] - f[a]
                total = term if total is None else total + term
        flux.append(total)
    return rho, flux


def project(vector, parts):
    total = None
    for dim in range(3):
        if vector[dim]:
            if total is None:
                total = parts[dim] if vector[dim] > 0 else -parts[dim]
            else:
                total = total + parts[dim] if vector[dim] > 0 else total - parts[dim]
    return total


def collide(f, rho, flux, force):
    factor = 1.0 - 0.5 / relax_time
    keep, gain = 1.0 - 1.0 / relax_time, 1.0 / relax_time
    mom = [flux[d] + 0.5 * force[d] for d in range(3)]
    inv = 1.0 / rho
    u = [mom[d] * inv for d in range(3)]
    usq = u[0] * mom[0] + u[1] * mom[1] + u[2] * mom[2]
    ug = u[0] * force[0] + u[1] * force[1] + u[2] * force[2]
    base = gain * (rho - 1.5 * usq) - (3.0 * factor) * ug
    post = [None] * 19
    post[0] = keep * f[0] + lattice_weight[0] * base
    for a, b in PAIRS:
        vector = velocity_set[a]
        cu, cm, cg = project(vector, u), project(vector, mom), project(vector, force)
        even = base + cu * ((4.5 * gain) * cm + (9.0 * factor) * cg)
        odd = (3.0 * gain) * cm + (3.0 * factor) * cg
        w = lattice_weight[a]
        post[a] = keep * f[a] + w * (even + odd)
        post[b] = keep * f[b] + w * (even - odd)
    return post


def split(a):
    hi = a.astype(BF16)
    return hi, (a - hi.astype(F32)).astype(BF16)


def dot(a, b):
    return jnp.dot(a, b, preferred_element_type=F32)


def dot_t(a, b):
    return lax.dot_general(a, b, (((1,), (1,)), ((), ())), preferred_element_type=F32)


def stacked(a):
    return jnp.concatenate(split(a), axis=0)


def dot_select(pick, b):
    h = b.astype(BF16)
    rest = b - h.astype(F32)
    m = rest.astype(BF16)
    l = (rest - m.astype(F32)).astype(BF16)
    return (dot(pick, h) + dot(pick, m)) + dot(pick, l)


def pattern(n):
    m = n & 3
    one, zero = jnp.float32(1.0), jnp.float32(0.0)
    c = jnp.where(m == 0, one, jnp.where(m == 2, -one, zero))
    s = jnp.where(m == 1, one, jnp.where(m == 3, -one, zero))
    return n.astype(F32), c, s


def weight(row, pat):
    x, c, s = row
    n, cp, sp = pat
    return jnp.where(jnp.abs(x - n) < 2.0, 0.25 + 0.25 * (c * cp + s * sp), 0.0)


def iota(shape, dim):
    return lax.broadcasted_iota(jnp.int32, shape, dim)


def kernel(nx, ny, pop_in, frac_in, spans_in, stiff_in, out_pop, out_vel,
           frac, spans, stiff, vel,
           fm, mo, fl, lf, gf, pm, fr_send, fr_all, data, sel_t, xyz, bend, wm, plane,
           ws, wx, wz_rows, brow, urow, vst, us, u_ret, u_recv,
           p_flow, fl_l, fl_r, sf, st, p1, r1l, r1r, gxa, gxb, daa, dab, dba, dbb,
           p2, r2l, r2r, d2aa, d2ab, d2ba, d2bb, xsp, xsm, xrp, xrm, gs,
           ag_s, ag_r, u_s, u_r, k_s, k_r, in_s, out_s):
    me_x, me_y = lax.axis_index("gx"), lax.axis_index("gy")
    east, west = lax.rem(me_x + 1, nx), lax.rem(me_x + nx - 1, nx)
    north, south = lax.rem(me_y + 1, ny), lax.rem(me_y + ny - 1, ny)
    tile_y = 256

    barrier = pltpu.get_barrier_semaphore()
    partners = [(me_x, lax.rem(me_y + d, ny)) for d in range(1, ny)]
    partners += [(east, me_y), (west, me_y), (east, north), (east, south), (west, north), (west, south)]
    for partner in partners:
        pl.semaphore_signal(barrier, inc=1, device_id=partner, device_id_type=MESH)

    def remote(src, dst, k, target):
        copy = pltpu.make_async_remote_copy(
            src_ref=src, dst_ref=dst, send_sem=k_s.at[k], recv_sem=k_r.at[k],
            device_id=target, device_id_type=MESH)
        copy.start()
        return copy

    lane, sub = iota((8, 128), 1), iota((8, 128), 0)
    cell, zl, xs = lane & 7, lane >> 3, sub & 3
    own = (sub >> 2) + (cell >> 2) == 1
    edge1 = ((sub < 4) & (lane == 0), (sub >= 4) & (lane == 127))
    edge4 = (lane >> 2) + (sub >> 2) * 32 == 0
    edge4 = edge4 | ((sub >= 4) & (lane >= 124))

    small = [pltpu.make_async_copy(a, b, in_s.at[4 + k])
             for k, (a, b) in enumerate(((frac_in, frac), (spans_in, spans), (stiff_in, stiff)))]
    for copy in small:
        copy.start()
    loads = []
    for q in range(4):
        part = pl.ds(4 * q, 4)
        loads.append(pltpu.make_async_copy(pop_in.at[:, part], fm.at[:, part], in_s.at[q]))
        loads[q].start()
    small[0].wait()
    for c in range(3):
        for f in range(2):
            fr_send[2 * c + f : 2 * c + f + 1, :] = frac[c, f : f + 1, :]
    fr_all[me_y] = fr_send[...]
    pl.semaphore_wait(barrier, len(partners))
    gathers = []
    for d in range(1, ny):
        copy = pltpu.make_async_remote_copy(
            src_ref=fr_send, dst_ref=fr_all.at[me_y], send_sem=ag_s.at[d], recv_sem=ag_r.at[d],
            device_id=(me_x, lax.rem(me_y + d, ny)), device_id_type=MESH)
        copy.start()
        gathers.append(copy)

    def first(z, carry):
        f = []
        for entry in range(19):
            f.append(lattice_weight[entry] + deviation_unit * fm[entry, z])
            fm[entry, z] = f[entry]
        rho, flux = moments(f)
        mo[0, z] = rho
        inv = 1.0 / rho
        for d in range(3):
            mo[1 + d, z] = flux[d]
            fl[d, z] = flux[d] * inv
        return carry

    for q in range(4):
        loads[q].wait()
        lax.fori_loop(4 * q, 4 * q + 4, first, 0)

    def pack(ref, n):
        def body(z, acc):
            rolled = pltpu.roll(ref[:, z], 8 * z + 4, 2)
            return jnp.where(zl[None] == z, rolled, acc)
        return lax.fori_loop(0, 16, body, jnp.zeros((n, 8, 128), F32))

    p_flow[...] = pack(fl, 3)
    flows = [remote(p_flow, fl_l, 0, (me_x, north)), remote(p_flow, fl_r, 1, (me_x, south))]
    small[1].wait()
    small[2].wait()

    st[...] = pack(fm, 19)

    def rows_of_flow():
        v = fl[...].reshape(3, 8, 2, 8, 128)
        a, b = v[:, :, 0].reshape(24, 8, 128), v[:, :, 1].reshape(24, 8, 128)
        low = (sub < 4)[None]
        halves = (jnp.where(low, a, pltpu.roll(b, 4, 1)), jnp.where(low, pltpu.roll(a, 4, 1), b))
        for k, half in enumerate(halves):
            hi, lo = split(half.reshape(192, 128))
            for at in (128 * k, 256 + 128 * k):
                lf[0:192, at : at + 128] = hi
                lf[192:384, at : at + 128] = lo

    rows_of_flow()

    span_cols = []
    row16, lane32 = iota((16, 32), 0), iota((16, 32), 1)
    for f in range(2):
        line = jnp.broadcast_to(spans[f : f + 1, :].astype(F32), (16, 32))
        for i in range(2):
            span_cols.append(jnp.sum(jnp.where(lane32 == 2 * row16 + i, line, 0.0), axis=1, keepdims=True))
    span_col = jnp.concatenate(span_cols + [jnp.full((64, 1), -1.0, F32)], axis=0)
    r128, l128 = iota((128, 128), 0), iota((128, 128), 1)
    target = me_y + (l128 >> 3) - 1
    target = jnp.where(target < 0, target + ny, jnp.where(target >= ny, target - ny, target)).astype(F32)
    match = jnp.where((jnp.broadcast_to(span_col, (128, 128)) == target) & (l128 < 24), 1.0, 0.0)
    before = jnp.where(l128 < r128, 1.0, 0.0).astype(BF16)
    rank = jnp.dot(before, match.astype(BF16), preferred_element_type=F32)
    chosen = jnp.where(rank == (l128 & 7).astype(F32), match, 0.0)
    sel_t[...] = chosen
    sel = chosen.T
    valid = jnp.sum(sel, axis=1, keepdims=True)[0:32]
    pick = sel[0:32].astype(BF16)

    for copy in gathers:
        copy.wait()
    anchor = (me_x * 4).astype(F32)
    l16, r16 = iota((16, 128), 1), iota((16, 128), 0)
    data[64:128, :] = jnp.zeros((64, 768), F32)
    for f in range(2):
        strength = stiff[f].astype(F32) * (stiff_unit / tile_y)
        for c in range(3):
            x = []
            for i in range(2):
                part = fr_all[:, 2 * c + f, i * 128 : (i + 1) * 128]
                if c == 0:
                    x.append((anchor + 1.0) + part * (4 - 3.01))
                elif c == 1:
                    x.append(span_cols[2 * f + i] * tile_y + part * tile_y)
                else:
                    x.append(1.0 + part * (16 - 3.01))
            ahead = [pltpu.roll(x[i], 127, 1) for i in range(2)]
            g0 = jnp.where(l16 == 127, ahead[1], ahead[0]) - x[0]
            g1 = jnp.where(l16 == 127, pltpu.roll(ahead[0], 15, 0), ahead[1]) - x[1]
            if c == 1:
                period = float(ny * tile_y)
                half = 0.5 * period
                g0 = jnp.where(g0 > half, g0 - period, jnp.where(g0 < -half, g0 + period, g0))
                g1 = jnp.where(g1 > half, g1 - period, jnp.where(g1 < -half, g1 + period, g1))
            g1 = jnp.where((l16 == 127) & (r16 == 15), 0.0, g1)
            b0, b1 = pltpu.roll(g0, 1, 1), pltpu.roll(g1, 1, 1)
            prev0 = jnp.where(l16 == 0, pltpu.roll(b1, 1, 0), b0)
            prev1 = jnp.where(l16 == 0, b0, b1)
            at = f * 32
            cols, more = slice(128 * c, 128 * c + 128), slice(384 + 128 * c, 512 + 128 * c)
            data[at : at + 16, cols] = x[0]
            data[at + 16 : at + 32, cols] = x[1]
            data[at : at + 16, more] = (g0 - prev0) * strength
            data[at + 16 : at + 32, more] = (g1 - prev1) * strength
    slots_of = dot_select(pick, data[...])
    for c in range(3):
        bend[c] = slots_of[:, 384 + 128 * c : 512 + 128 * c]
        x = slots_of[:, 128 * c : 128 * c + 128]
        if c == 0:
            x = x - anchor
        elif c == 1:
            x = x - (me_y * tile_y).astype(F32)
            period = float(ny * tile_y)
            x = jnp.where(x > 0.5 * period, x - period, jnp.where(x < -0.5 * period, x + period, x))
            x = jnp.where(valid > 0.5, x, 1.0e6)
        base = jnp.floor(x)
        part = (0.5 * math.pi) * (x - base)
        cos, sin = jnp.cos(part), jnp.sin(part)
        turn = base - 4.0 * jnp.floor(0.25 * base)
        xyz[c, 0] = x
        xyz[c, 1] = jnp.where(turn == 0.0, cos, jnp.where(turn == 1.0, -sin, jnp.where(turn == 2.0, -cos, sin)))
        xyz[c, 2] = jnp.where(turn == 0.0, sin, jnp.where(turn == 1.0, cos, jnp.where(turn == 2.0, -sin, -cos)))

    pat_z = pattern(iota((16, 128), 0))
    pat_low, pat_high = pattern(sub - 4), pattern(sub + (tile_y - 4))
    pat_x, pat_y = pattern(xs), pattern(sub)
    down = iota((16, 128), 0).astype(F32)

    def weights(s, carry):
        def line(group, c):
            return [xyz[c, k, pl.ds(group * 8 + s, 1), :] for k in range(3)]
        where_s = pl.ds(pl.multiple_of(s * 128, 128), 128)

        for group in range(3):
            lx, ly, lz = line(group, 0), line(group, 1), line(group, 2)
            across = weight(lx, pat_x)
            wx[group, :, where_s] = across
            wz_rows[group] = weight(lz, pat_z)
            wz = [jnp.broadcast_to(wz_rows[group, z : z + 1, :], (8, 128)) for z in range(16)]
            for slot, pat in ((0, pat_low), (1, pat_high), (2, pat_low), (3, pat_high)):
                if (group, slot) not in ((0, 0), (2, 1), (1, 2), (1, 3)):
                    continue
                columns = pl.ds(pl.multiple_of(slot * 1024 + s * 128, 128), 128)
                wy = weight(ly, pat)
                for z in range(0, 16, 2):
                    hi, lo = split(jnp.concatenate([wz[z] * wy, wz[z + 1] * wy], axis=0))
                    ws[8 * z : 8 * z + 16, columns] = hi
                    ws[128 + 8 * z : 144 + 8 * z, columns] = lo
            if group == 1:
                tall = 0.25 + 0.25 * (ly[1] * pat_y[1] + ly[2] * pat_y[2])
                hi8 = tall.astype(BF16).astype(F32)
                hi, lo = jnp.concatenate([hi8, hi8], axis=0), jnp.concatenate([tall - hi8, tall - hi8], axis=0)
                gap = ly[0] - down
                for r in range(16):
                    near = jnp.abs(gap - 16.0 * r) < 2.0
                    wm[16 * r : 16 * r + 16, where_s] = jnp.where(near, hi, 0.0).astype(BF16)
                    wm[256 + 16 * r : 272 + 16 * r, where_s] = jnp.where(near, lo, 0.0).astype(BF16)
                for i in range(8):
                    plane[8 * i : 8 * i + 8, where_s] = jnp.where(sub < 4, wz[2 * i], wz[2 * i + 1]) * across
            for c in range(3):
                brow[group, c : c + 1, where_s] = bend[c, pl.ds(group * 8 + s, 1), :]
        return carry

    lax.fori_loop(0, 8, weights, 0)
    for group in range(3):
        brow[group, 3:8, :] = jnp.zeros((5, 1024), F32)

    def merge(centre, left, right):
        n = centre.shape[0]
        side = jnp.where((cell < 4)[None], left, right)
        return jnp.where(own[None], centre, pltpu.roll(side, 4, 1))

    left_side = jnp.where(iota((8, 1024), 0) < 4, 1.0, 0.0)
    right_side = 1.0 - left_side

    def interpolate_spread():
        blank = jnp.zeros((8, 128), F32)
        full = stacked(jnp.concatenate([sf[0], sf[1], sf[2], blank], axis=0))
        halo = stacked(jnp.concatenate([jnp.where(own, 0.0, sf[d]) for d in range(3)] + [blank], axis=0))
        near = dot(jnp.concatenate([full, full], axis=1), ws[:, 0:2048])
        mine = dot(jnp.concatenate([halo, halo], axis=1), ws[:, 2048:4096])
        for c in range(3):
            a = near[8 * c : 8 * c + 8] + near[32 + 8 * c : 40 + 8 * c]
            b = mine[8 * c : 8 * c + 8] + mine[32 + 8 * c : 40 + 8 * c]
            urow[0, c : c + 1, :] = jnp.sum(a[:, 0:1024] * (wx[0] * left_side), axis=0, keepdims=True)
            urow[2, c : c + 1, :] = jnp.sum(a[:, 1024:2048] * (wx[2] * right_side), axis=0, keepdims=True)
            both = b[:, 0:1024] * left_side + b[:, 1024:2048] * right_side
            urow[1, c : c + 1, :] = jnp.sum(both * wx[1], axis=0, keepdims=True)
        for q in range(4):
            cols = slice(256 * q, 256 * q + 256)
            a = dot(lf[...], wm[:, cols])
            for c in range(3):
                both = a[64 * c : 64 * c + 64] + a[192 + 64 * c : 256 + 64 * c]
                part = jnp.sum(both * plane[:, cols], axis=0, keepdims=True)
                urow[1, c : c + 1, cols] = urow[1, c : c + 1, cols] + part

    def forces():
        return [brow[group] - feedback_gain * urow[group] for group in range(3)]

    def spread_strips(force):
        total = None
        for slot, (group, side) in enumerate(((0, left_side), (2, right_side), (1, left_side), (1, right_side))):
            w = wx[group] * side
            v = jnp.concatenate([force[group][c : c + 1] * w for c in range(3)] + [jnp.zeros((8, 1024), F32)], axis=0)
            cols = slice(1024 * slot, 1024 * slot + 1024)
            part = dot_t(stacked(v), ws[:, cols])
            part = (part[0:32, 0:128] + part[0:32, 128:256]) + part[32:64, 0:128]
            total = part if total is None else total + part
        return [total[8 * c : 8 * c + 8] for c in range(3)]

    def spread_tile(force):
        for q in range(8):
            cols = slice(128 * q, 128 * q + 128)
            for c in range(3):
                hi, lo = split(force[1][c : c + 1, cols] * plane[:, cols])
                vst[64 * c : 64 * c + 64, cols] = hi
                vst[192 + 64 * c : 256 + 64 * c, cols] = lo
        total = dot_t(vst[...], wm[...])
        total = (total[0:192, 0:256] + total[0:192, 256:512]) + total[192:384, 0:256]
        a, b = total[:, 0:128].reshape(24, 8, 128), total[:, 128:256].reshape(24, 8, 128)
        low = (sub < 4)[None]
        even = jnp.where(low, a, pltpu.roll(b, 4, 1)).reshape(24, 1, 8, 128)
        odd = jnp.where(low, pltpu.roll(a, 4, 1), b).reshape(24, 1, 8, 128)
        gf[...] = jnp.concatenate([even, odd], axis=1).reshape(3, 16, 8, 128)

    def collide_tile(step):
        def body(q, carry):
            to_east, to_west = [None] * 5, [None] * 5
            for zz in range(4):
                z = 4 * q + zz
                f = [fm[entry, z] for entry in range(19)]
                force = []
                for d in range(3):
                    force.append(jnp.where(edge4, pltpu.roll(gs[d], 124 - 8 * z, 1), gf[d, z]))
                post = collide(f, mo[0, z], [mo[1, z], mo[2, z], mo[3, z]], force)
                for entry in range(19):
                    pm[entry, z] = post[entry]
                for k in range(5):
                    a = pltpu.roll(post[EAST[k]], 5 + zz, 0) if zz < 3 else post[EAST[k]]
                    b = pltpu.roll(post[WEST[k]], zz, 0) if zz else post[WEST[k]]
                    to_east[k] = jnp.where(xs == zz, a, to_east[k]) if zz else a
                    to_west[k] = jnp.where(xs == zz, b, to_west[k]) if zz else b
            for k in range(5):
                xsp[step, q, k] = to_east[k]
                xsm[step, q, k] = to_west[k]
            row_copy(step, 0, q).start()
            row_copy(step, 1, q).start()
            return carry
        lax.fori_loop(0, 4, body, 0)

    def row_copy(step, way, q):
        src, dst, target = ((xsp, xrp, (east, me_y)), (xsm, xrm, (west, me_y)))[way]
        k = 18 + 8 * step + 4 * way + q
        return pltpu.make_async_remote_copy(
            src_ref=src.at[step, q], dst_ref=dst.at[step, q], send_sem=k_s.at[k], recv_sem=k_r.at[k],
            device_id=target, device_id_type=MESH)

    def stream_strips(strip, ext_east, ext_west):
        result = {}
        for entry in strip["want"]:
            cx, cy, cz = velocity_set[entry]
            v = strip[entry]
            if cx == 1:
                v = jnp.where(xs == 0, ext_east[entry], pltpu.roll(v, 1, 0))
            elif cx == -1:
                v = jnp.where(xs == 3, ext_west[entry], pltpu.roll(v, 7, 0))
            turn = (8 * cz + cy) % 128
            if turn:
                v = pltpu.roll(v, turn, 1)
            if cz == 1:
                v = jnp.where(zl == 0, strip[opposite(entry)], v)
            elif cz == -1:
                v = jnp.where(zl == 15, strip[opposite(entry)], v)
            result[entry] = v
        return result

    def stream_at(entry, z, step):
        cx, cy, cz = velocity_set[entry]
        zs = jnp.maximum(z - 1, 0) if cz == 1 else jnp.minimum(z + 1, 15) if cz == -1 else z
        v = pm[entry, zs]
        if cx:
            zz = zs & 3
            if cx == 1:
                row = pltpu.roll(xrp[step, zs >> 2, EAST.index(entry)], (8 - zz) & 7, 0)
                v = jnp.where(xs == 0, row, pltpu.roll(v, 1, 0))
            else:
                row = pltpu.roll(xrm[step, zs >> 2, WEST.index(entry)], 3 - zz, 0)
                v = jnp.where(xs == 3, row, pltpu.roll(v, 7, 0))
        if cy:
            r = pltpu.roll(v, 1 if cy == 1 else 127, 1)
            v = jnp.where(lane == (0 if cy == 1 else 127), pltpu.roll(r, 4, 0), r)
        if cz:
            v = jnp.where(z == (0 if cz == 1 else 15), pm[opposite(entry), z], v)
        if cy:
            strip = pltpu.roll(st[entry], 124 - 8 * z, 1)
            v = jnp.where(edge1[0] if cy == 1 else edge1[1], strip, v)
        return v

    for copy in flows:
        copy.wait()
    sf[...] = merge(p_flow[...], fl_l[...], fl_r[...])
    interpolate_spread()
    force = forces()
    strip_force = spread_strips(force)
    for d in range(3):
        gs[d] = strip_force[d]
    f = [st[entry] for entry in range(19)]
    rho, flux = moments(f)
    post = collide(f, rho, flux, strip_force)
    for k, entry in enumerate(STRIP):
        p1[k] = post[entry]
    strips = [
        remote(p1, r1l, 2, (me_x, north)),
        remote(p1, r1r, 3, (me_x, south)),
        remote(p1.at[0:5], gxa, 4, (east, me_y)),
        remote(p1.at[8:13], gxb, 5, (west, me_y)),
        remote(p1.at[0:5], daa, 6, (east, north)),
        remote(p1.at[0:5], dab, 7, (east, south)),
        remote(p1.at[8:13], dba, 8, (west, north)),
        remote(p1.at[8:13], dbb, 9, (west, south)),
    ]
    spread_tile(force)
    collide_tile(0)
    rows = [row_copy(0, way, q) for way in range(2) for q in range(4)]

    for copy in strips:
        copy.wait()
    whole = merge(p1[...], r1l[...], r1r[...])
    beside_w = pltpu.roll(merge(gxa[...], daa[...], dab[...]), 5, 1)
    beside_e = pltpu.roll(merge(gxb[...], dba[...], dbb[...]), 3, 1)
    strip = {entry: whole[AT[entry]] for entry in range(19)}
    strip["want"] = range(19)
    moved = stream_strips(strip, {e: beside_w[k] for k, e in enumerate(EAST)},
                          {e: beside_e[k] for k, e in enumerate(WEST)})
    for entry in range(19):
        st[entry] = moved[entry]
    f = [moved[entry] for entry in range(19)]
    strip_rho, strip_flux = moments(f)
    inv = 1.0 / strip_rho
    for d in range(3):
        sf[d] = strip_flux[d] * inv
    for copy in rows:
        copy.wait()

    def second(z, carry):
        f = []
        for entry in range(19):
            v = stream_at(entry, z, 0)
            f.append(v)
            fm[entry, z] = v
        rho, flux = moments(f)
        mo[0, z] = rho
        inv = 1.0 / rho
        for d in range(3):
            mo[1 + d, z] = flux[d]
            fl[d, z] = flux[d] * inv
        return carry

    lax.fori_loop(0, 16, second, 0)
    rows_of_flow()

    interpolate_spread()
    force = forces()
    strip_force = spread_strips(force)
    for d in range(3):
        gs[d] = strip_force[d]
    f = [st[entry] for entry in range(19)]
    post = collide(f, strip_rho, strip_flux, strip_force)
    for k, entry in enumerate(STRIP):
        p2[k] = post[entry]
    strips = [
        remote(p2.at[4:9], r2l, 12, (me_x, north)),
        remote(p2.at[12:17], r2r, 13, (me_x, south)),
        remote(p2.at[4:5], d2aa, 14, (east, north)),
        remote(p2.at[0:1], d2ab, 15, (east, south)),
        remote(p2.at[8:9], d2ba, 16, (west, north)),
        remote(p2.at[12:13], d2bb, 17, (west, south)),
    ]
    us[...] = jnp.zeros((128, 384), F32)
    for s in range(8):
        for c in range(3):
            us[8 + s : 9 + s, 128 * c : 128 * c + 128] = urow[1, c : c + 1, 128 * s : 128 * s + 128]
    home = sel_t[0:64].astype(BF16)
    homeward = dot_select(home, us[...])
    for c in range(3):
        back = homeward[:, 128 * c : 128 * c + 128]
        for f in range(2):
            for i in range(2):
                at = (2 * f + i) * 16
                u_ret[:, 2 * c + f, i * 128 : (i + 1) * 128] = back[at : at + 16]
    u_recv[me_y] = u_ret[me_y]
    returns = []
    for d in range(1, ny):
        peer = lax.rem(me_y + d, ny)
        copy = pltpu.make_async_remote_copy(
            src_ref=u_ret.at[peer], dst_ref=u_recv.at[me_y], send_sem=u_s.at[d], recv_sem=u_r.at[d],
            device_id=(me_x, peer), device_id_type=MESH)
        copy.start()
        returns.append(copy)

    spread_tile(force)
    collide_tile(1)
    rows = [row_copy(1, way, q) for way in range(2) for q in range(4)]

    for copy in strips:
        copy.wait()
    own_strip = {entry: p2[AT[entry]] for entry in range(19)}
    for k, entry in enumerate(STRIP[4:9]):
        own_strip[entry] = jnp.where(own, p2[AT[entry]], pltpu.roll(r2l[k], 4, 0))
    south_side = dict(own_strip)
    for k, entry in enumerate(STRIP[12:17]):
        south_side[entry] = jnp.where(own, p2[AT[entry]], pltpu.roll(r2r[k], 4, 0))
    south_side["want"] = STRIP[4:9] + STRIP[12:17]
    for k, entry in enumerate(STRIP[4:9]):
        south_side[entry] = own_strip[entry]
    moved = stream_strips(
        south_side,
        {7: pltpu.roll(d2aa[0], 1, 0), 9: pltpu.roll(d2ab[0], 1, 0)},
        {10: pltpu.roll(d2ba[0], 7, 0), 8: pltpu.roll(d2bb[0], 7, 0)})
    for entry in south_side["want"]:
        st[entry] = moved[entry]
    for copy in rows:
        copy.wait()

    def last(z, carry):
        for entry in range(19):
            v = stream_at(entry, z, 1)
            out_pop[entry, z] = (v - lattice_weight[entry]) * (1.0 / deviation_unit)
        return carry

    lax.fori_loop(0, 16, last, 0)
    for copy in returns:
        copy.wait()
    total = u_recv[0]
    for j in range(1, ny):
        total = total + u_recv[j]
    total = total / deviation_unit
    for c in range(3):
        for f in range(2):
            out_vel[c, f : f + 1, :] = total[2 * c + f : 2 * c + f + 1, :]


def per_device(nx, ny, populations, fraction, spans, stiffness):
    pop = populations.reshape(19, 16, 4, 2, 128).transpose(0, 1, 3, 2, 4).reshape(19, 16, 8, 128)
    anywhere = pl.BlockSpec(memory_space=pl.ANY)
    V = lambda *shape: pltpu.VMEM(shape, F32)
    B = lambda *shape: pltpu.VMEM(shape, BF16)
    dma = pltpu.SemaphoreType.DMA
    tile = V(19, 16, 8, 128)
    scratch = [
        V(3, 2, 256), pltpu.VMEM((2, 32), jnp.int32), pltpu.SMEM((2,), jnp.int32), V(3, 2, 256),
        tile, V(4, 16, 8, 128), V(3, 16, 8, 128), B(384, 512), V(3, 16, 8, 128), tile,
        V(6, 256), V(ny, 6, 256), V(128, 768), V(128, 128), V(3, 3, 32, 128), V(3, 32, 128),
        B(512, 1024), V(64, 1024), B(256, 4096), V(3, 8, 1024), V(3, 16, 128),
        V(3, 8, 1024), V(3, 8, 1024), B(384, 1024), V(128, 384), V(ny, 6, 256), V(ny, 6, 256),
        V(3, 8, 128), V(3, 8, 128), V(3, 8, 128), V(3, 8, 128), V(19, 8, 128),
        V(20, 8, 128), V(20, 8, 128), V(20, 8, 128),
        V(5, 8, 128), V(5, 8, 128), V(5, 8, 128), V(5, 8, 128), V(5, 8, 128), V(5, 8, 128),
        V(20, 8, 128), V(5, 8, 128), V(5, 8, 128), V(1, 8, 128), V(1, 8, 128), V(1, 8, 128), V(1, 8, 128),
        V(2, 4, 5, 8, 128), V(2, 4, 5, 8, 128), V(2, 4, 5, 8, 128), V(2, 4, 5, 8, 128), V(3, 8, 128),
        dma((ny,)), dma((ny,)), dma((ny,)), dma((ny,)), dma((34,)), dma((34,)), dma((7,)), dma((5,)),
    ]
    out, vel = pl.pallas_call(
        functools.partial(kernel, nx, ny),
        out_shape=(jax.ShapeDtypeStruct((19, 16, 8, 128), F32), jax.ShapeDtypeStruct((3, 2, 256), F32)),
        in_specs=[pl.BlockSpec(memory_space=pltpu.HBM)] * 4,
        out_specs=(pl.BlockSpec(memory_space=pltpu.VMEM),) * 2,
        scratch_shapes=scratch,
        name="lattice",
        compiler_params=pltpu.CompilerParams(
            collective_id=0, has_side_effects=True, vmem_limit_bytes=40 << 20),
    )(*[pltpu.with_memory_space_constraint(x, pltpu.HBM) for x in (
        pop, fraction.transpose(1, 0, 2), spans.reshape(spans.shape[0], spans.shape[1]), stiffness)])
    out = out.reshape(19, 16, 2, 4, 128).transpose(0, 1, 3, 2, 4).reshape(19, 16, 4, 256)
    return out, vel.transpose(1, 0, 2)


def solution(mesh):
    placed = (P(None, None, "gx", "gy"), P("gx", None, "gy"), P("gx", None, None), P("gx"))
    return jax.shard_map(
        functools.partial(per_device, mesh.shape["gx"], mesh.shape["gy"]),
        mesh=mesh,
        in_specs=placed,
        out_specs=(P(None, None, "gx", "gy"), P("gx", None, "gy")),
        check_vma=False,
    )
```

```python
import functools
import math

import jax
import jax.numpy as jnp
from jax import lax
from jax.experimental import pallas as pl
from jax.experimental.pallas import tpu as pltpu
from jax.sharding import PartitionSpec as P

F32 = jnp.float32
BF16 = jnp.bfloat16
MESH = pl.DeviceIdType.MESH

velocity_set = (
    (0, 0, 0), (1, 0, 0), (-1, 0, 0), (0, 1, 0), (0, -1, 0), (0, 0, 1), (0, 0, -1),
    (1, 1, 0), (-1, -1, 0), (1, -1, 0), (-1, 1, 0), (1, 0, 1), (-1, 0, -1),
    (1, 0, -1), (-1, 0, 1), (0, 1, 1), (0, -1, -1), (0, 1, -1), (0, -1, 1),
)
lattice_weight = (1.0 / 3.0,) + (1.0 / 18.0,) * 6 + (1.0 / 36.0,) * 12
relax_time = 0.8
deviation_unit = 0.002
feedback_gain = 2.0
stiff_unit = 0.002

STRIP = (9, 1, 11, 13, 7, 3, 15, 17, 10, 2, 12, 14, 8, 4, 16, 18, 9, 0, 5, 6)
AT = {entry: STRIP.index(entry) for entry in range(19)}
EAST, WEST = STRIP[0:5], STRIP[8:13]
STRAIGHT = tuple(e for e in range(19) if velocity_set[e][0] == 0)
SLANTED = EAST + WEST
EDGED = tuple(e for e in range(19) if velocity_set[e][1] != 0)
PAIRS = tuple((i, i + 1) for i in range(1, 19, 2))


def opposite(entry):
    return entry + 1 if entry % 2 == 1 else entry - 1


def moments(f):
    rho = f[0]
    for entry in range(1, 19):
        rho = rho + f[entry]
    flux = []
    for dim in range(3):
        total = None
        for a, b in PAIRS:
            c = velocity_set[a][dim]
            if c:
                term = f[a] - f[b] if c > 0 else f[b] - f[a]
                total = term if total is None else total + term
        flux.append(total)
    return rho, flux


def project(vector, parts):
    total = None
    for dim in range(3):
        if vector[dim]:
            if total is None:
                total = parts[dim] if vector[dim] > 0 else -parts[dim]
            else:
                total = total + parts[dim] if vector[dim] > 0 else total - parts[dim]
    return total


def collide(f, rho, flux, force):
    factor = 1.0 - 0.5 / relax_time
    keep, gain = 1.0 - 1.0 / relax_time, 1.0 / relax_time
    mom = [flux[d] + 0.5 * force[d] for d in range(3)]
    inv = 1.0 / rho
    u = [mom[d] * inv for d in range(3)]
    usq = u[0] * mom[0] + u[1] * mom[1] + u[2] * mom[2]
    ug = u[0] * force[0] + u[1] * force[1] + u[2] * force[2]
    base = gain * (rho - 1.5 * usq) - (3.0 * factor) * ug
    post = [None] * 19
    post[0] = keep * f[0] + lattice_weight[0] * base
    for a, b in PAIRS:
        vector = velocity_set[a]
        cu, cm, cg = project(vector, u), project(vector, mom), project(vector, force)
        even = base + cu * ((4.5 * gain) * cm + (9.0 * factor) * cg)
        odd = (3.0 * gain) * cm + (3.0 * factor) * cg
        w = lattice_weight[a]
        post[a] = keep * f[a] + w * (even + odd)
        post[b] = keep * f[b] + w * (even - odd)
    return post


def split(a):
    hi = a.astype(BF16)
    return hi, (a - hi.astype(F32)).astype(BF16)


def dot(a, b):
    return jnp.dot(a, b, preferred_element_type=F32)


def dot_t(a, b):
    return lax.dot_general(a, b, (((1,), (1,)), ((), ())), preferred_element_type=F32)


def stacked(a):
    return jnp.concatenate(split(a), axis=0)


def dot_select(pick, b):
    h = b.astype(BF16)
    rest = b - h.astype(F32)
    m = rest.astype(BF16)
    l = (rest - m.astype(F32)).astype(BF16)
    return (dot(pick, h) + dot(pick, m)) + dot(pick, l)


def pattern(n):
    m = n & 3
    one, zero = jnp.float32(1.0), jnp.float32(0.0)
    c = jnp.where(m == 0, one, jnp.where(m == 2, -one, zero))
    s = jnp.where(m == 1, one, jnp.where(m == 3, -one, zero))
    return n.astype(F32), c, s


def weight(row, pat):
    x, c, s = row
    n, cp, sp = pat
    return jnp.where(jnp.abs(x - n) < 2.0, 0.25 + 0.25 * (c * cp + s * sp), 0.0)


def iota(shape, dim):
    return lax.broadcasted_iota(jnp.int32, shape, dim)


def kernel(nx, ny, pop_in, frac_in, spans_in, stiff_in, out_pop, out_vel,
           frac, spans, stiff, vel,
           fm, mo, fl, lf, gf, pm, fr_send, fr_all, data, sel_t, xyz, bend, wm, plane,
           ws, wx, wz_rows, brow, urow, vst, us, u_ret, u_recv,
           p_flow, fl_l, fl_r, sf, st, p1, pn, ps, pe, pw, r1l, r1r, gxa, gxb, daa, dab, dba, dbb,
           p2, r2l, r2r, d2aa, d2ab, d2ba, d2bb, xsp, xsm, xrp, xrm, gs,
           ag_s, ag_r, u_s, u_r, k_s, k_r, in_s, out_s):
    me_x, me_y = lax.axis_index("gx"), lax.axis_index("gy")
    east, west = lax.rem(me_x + 1, nx), lax.rem(me_x + nx - 1, nx)
    north, south = lax.rem(me_y + 1, ny), lax.rem(me_y + ny - 1, ny)
    tile_y = 256

    barrier = pltpu.get_barrier_semaphore()
    partners = [(me_x, lax.rem(me_y + d, ny)) for d in range(1, ny)]
    partners += [(east, me_y), (west, me_y), (east, north), (east, south), (west, north), (west, south)]
    for partner in partners:
        pl.semaphore_signal(barrier, inc=1, device_id=partner, device_id_type=MESH)

    def remote(src, dst, k, target):
        copy = pltpu.make_async_remote_copy(
            src_ref=src, dst_ref=dst, send_sem=k_s.at[k], recv_sem=k_r.at[k],
            device_id=target, device_id_type=MESH)
        copy.start()
        return copy

    lane, sub = iota((8, 128), 1), iota((8, 128), 0)
    cell, zl, xs = lane & 7, lane >> 3, sub & 3
    own = (sub >> 2) + (cell >> 2) == 1
    edge1 = ((sub < 4) & (lane == 0), (sub >= 4) & (lane == 127))
    edge4 = (lane >> 2) + (sub >> 2) * 32 == 0
    edge4 = edge4 | ((sub >= 4) & (lane >= 124))

    small = [pltpu.make_async_copy(a, b, in_s.at[4 + k])
             for k, (a, b) in enumerate(((frac_in, frac), (spans_in, spans), (stiff_in, stiff)))]
    for copy in small:
        copy.start()
    loads = []
    for q in range(4):
        part = pl.ds(4 * q, 4)
        loads.append(pltpu.make_async_copy(pop_in.at[:, part], fm.at[:, part], in_s.at[q]))
        loads[q].start()
    small[0].wait()
    for c in range(3):
        for f in range(2):
            fr_send[2 * c + f : 2 * c + f + 1, :] = frac[c, f : f + 1, :]
    fr_all[me_y] = fr_send[...]
    pl.semaphore_wait(barrier, len(partners))
    gathers = []
    for d in range(1, ny):
        copy = pltpu.make_async_remote_copy(
            src_ref=fr_send, dst_ref=fr_all.at[me_y], send_sem=ag_s.at[d], recv_sem=ag_r.at[d],
            device_id=(me_x, lax.rem(me_y + d, ny)), device_id_type=MESH)
        copy.start()
        gathers.append(copy)

    def first(z, carry):
        f = []
        for entry in range(19):
            f.append(lattice_weight[entry] + deviation_unit * fm[entry, z])
            fm[entry, z] = f[entry]
        rho, flux = moments(f)
        mo[0, z] = rho
        inv = 1.0 / rho
        for d in range(3):
            mo[1 + d, z] = flux[d]
            fl[d, z] = flux[d] * inv
        return carry

    for q in range(4):
        loads[q].wait()
        lax.fori_loop(4 * q, 4 * q + 4, first, 0)

    def pack(ref, n):
        def body(z, acc):
            rolled = pltpu.roll(ref[:, z], 8 * z + 4, 2)
            return jnp.where(zl[None] == z, rolled, acc)
        return lax.fori_loop(0, 16, body, jnp.zeros((n, 8, 128), F32))

    p_flow[...] = pack(fl, 3)
    flows = [remote(p_flow, fl_l, 0, (me_x, north)), remote(p_flow, fl_r, 1, (me_x, south))]
    small[1].wait()
    small[2].wait()

    st[...] = pack(fm, 19)

    def rows_of_flow():
        v = fl[...].reshape(3, 8, 2, 8, 128)
        a, b = v[:, :, 0].reshape(24, 8, 128), v[:, :, 1].reshape(24, 8, 128)
        low = (sub < 4)[None]
        halves = (jnp.where(low, a, pltpu.roll(b, 4, 1)), jnp.where(low, pltpu.roll(a, 4, 1), b))
        for k, half in enumerate(halves):
            hi, lo = split(half.reshape(192, 128))
            lf[0:192, 128 * k : 128 * k + 128] = hi
            lf[192:384, 128 * k : 128 * k + 128] = lo

    rows_of_flow()

    span_cols = []
    row16, lane32 = iota((16, 32), 0), iota((16, 32), 1)
    for f in range(2):
        line = jnp.broadcast_to(spans[f : f + 1, :].astype(F32), (16, 32))
        for i in range(2):
            span_cols.append(jnp.sum(jnp.where(lane32 == 2 * row16 + i, line, 0.0), axis=1, keepdims=True))
    span_col = jnp.concatenate(span_cols + [jnp.full((64, 1), -1.0, F32)], axis=0)
    r128, l128 = iota((128, 128), 0), iota((128, 128), 1)
    target = me_y + (l128 >> 3) - 1
    target = jnp.where(target < 0, target + ny, jnp.where(target >= ny, target - ny, target)).astype(F32)
    match = jnp.where((jnp.broadcast_to(span_col, (128, 128)) == target) & (l128 < 24), 1.0, 0.0)
    before = jnp.where(l128 < r128, 1.0, 0.0).astype(BF16)
    rank = jnp.dot(before, match.astype(BF16), preferred_element_type=F32)
    chosen = jnp.where(rank == (l128 & 7).astype(F32), match, 0.0)
    sel_t[...] = chosen
    sel = chosen.T
    valid = jnp.sum(sel, axis=1, keepdims=True)[0:32]
    pick = sel[0:32].astype(BF16)

    for copy in gathers:
        copy.wait()
    anchor = (me_x * 4).astype(F32)
    l16, r16 = iota((16, 128), 1), iota((16, 128), 0)
    data[64:128, :] = jnp.zeros((64, 768), F32)
    for f in range(2):
        strength = stiff[f].astype(F32) * (stiff_unit / tile_y)
        for c in range(3):
            x = []
            for i in range(2):
                part = fr_all[:, 2 * c + f, i * 128 : (i + 1) * 128]
                if c == 0:
                    x.append((anchor + 1.0) + part * (4 - 3.01))
                elif c == 1:
                    x.append(span_cols[2 * f + i] * tile_y + part * tile_y)
                else:
                    x.append(1.0 + part * (16 - 3.01))
            ahead = [pltpu.roll(x[i], 127, 1) for i in range(2)]
            g0 = jnp.where(l16 == 127, ahead[1], ahead[0]) - x[0]
            g1 = jnp.where(l16 == 127, pltpu.roll(ahead[0], 15, 0), ahead[1]) - x[1]
            if c == 1:
                period = float(ny * tile_y)
                half = 0.5 * period
                g0 = jnp.where(g0 > half, g0 - period, jnp.where(g0 < -half, g0 + period, g0))
                g1 = jnp.where(g1 > half, g1 - period, jnp.where(g1 < -half, g1 + period, g1))
            g1 = jnp.where((l16 == 127) & (r16 == 15), 0.0, g1)
            b0, b1 = pltpu.roll(g0, 1, 1), pltpu.roll(g1, 1, 1)
            prev0 = jnp.where(l16 == 0, pltpu.roll(b1, 1, 0), b0)
            prev1 = jnp.where(l16 == 0, b0, b1)
            at = f * 32
            cols, more = slice(128 * c, 128 * c + 128), slice(384 + 128 * c, 512 + 128 * c)
            data[at : at + 16, cols] = x[0]
            data[at + 16 : at + 32, cols] = x[1]
            data[at : at + 16, more] = (g0 - prev0) * strength
            data[at + 16 : at + 32, more] = (g1 - prev1) * strength
    slots_of = dot_select(pick, data[...])
    for c in range(3):
        bend[c] = slots_of[:, 384 + 128 * c : 512 + 128 * c]
        x = slots_of[:, 128 * c : 128 * c + 128]
        if c == 0:
            x = x - anchor
        elif c == 1:
            x = x - (me_y * tile_y).astype(F32)
            period = float(ny * tile_y)
            x = jnp.where(x > 0.5 * period, x - period, jnp.where(x < -0.5 * period, x + period, x))
            x = jnp.where(valid > 0.5, x, 1.0e6)
        base = jnp.floor(x)
        part = (0.5 * math.pi) * (x - base)
        cos, sin = jnp.cos(part), jnp.sin(part)
        turn = base - 4.0 * jnp.floor(0.25 * base)
        xyz[c, 0] = x
        xyz[c, 1] = jnp.where(turn == 0.0, cos, jnp.where(turn == 1.0, -sin, jnp.where(turn == 2.0, -cos, sin)))
        xyz[c, 2] = jnp.where(turn == 0.0, sin, jnp.where(turn == 1.0, cos, jnp.where(turn == 2.0, -sin, -cos)))

    pat_z = pattern(iota((16, 128), 0))
    pat_low, pat_high = pattern(sub - 4), pattern(sub + (tile_y - 4))
    pat_own = pattern(jnp.where(sub < 4, sub - 4, sub + (tile_y - 4)))
    pat_x, pat_y = pattern(xs), pattern(sub)
    down = iota((16, 128), 0).astype(F32)

    def weights(s, carry):
        def line(group, c):
            return [xyz[c, k, pl.ds(group * 8 + s, 1), :] for k in range(3)]
        where_s = pl.ds(pl.multiple_of(s * 128, 128), 128)

        for group in range(3):
            lx, ly, lz = line(group, 0), line(group, 1), line(group, 2)
            across = weight(lx, pat_x)
            wx[group, :, where_s] = across
            wz_rows[group] = weight(lz, pat_z)
            wz = [jnp.broadcast_to(wz_rows[group, z : z + 1, :], (8, 128)) for z in range(16)]
            columns = pl.ds(pl.multiple_of(group * 1024 + s * 128, 128), 128)
            wy = weight(ly, (pat_low, pat_own, pat_high)[group])
            for z in range(0, 16, 2):
                hi, lo = split(jnp.concatenate([wz[z] * wy, wz[z + 1] * wy], axis=0))
                ws[8 * z : 8 * z + 16, columns] = hi
                ws[128 + 8 * z : 144 + 8 * z, columns] = lo
            if group == 1:
                tall = 0.25 + 0.25 * (ly[1] * pat_y[1] + ly[2] * pat_y[2])
                hi8 = tall.astype(BF16).astype(F32)
                hi, lo = jnp.concatenate([hi8, hi8], axis=0), jnp.concatenate([tall - hi8, tall - hi8], axis=0)
                gap = ly[0] - down
                for r in range(16):
                    near = jnp.abs(gap - 16.0 * r) < 2.0
                    wm[16 * r : 16 * r + 16, where_s] = jnp.where(near, hi, 0.0).astype(BF16)
                    wm[256 + 16 * r : 272 + 16 * r, where_s] = jnp.where(near, lo, 0.0).astype(BF16)
                for i in range(8):
                    plane[8 * i : 8 * i + 8, where_s] = jnp.where(sub < 4, wz[2 * i], wz[2 * i + 1]) * across
            for c in range(3):
                brow[group, c : c + 1, where_s] = bend[c, pl.ds(group * 8 + s, 1), :]
        return carry

    lax.fori_loop(0, 8, weights, 0)
    for group in range(3):
        brow[group, 3:8, :] = jnp.zeros((5, 1024), F32)

    def merge(centre, left, right):
        n = centre.shape[0]
        side = jnp.where((cell < 4)[None], left, right)
        return jnp.where(own[None], centre, pltpu.roll(side, 4, 1))

    left_side = jnp.where(iota((8, 1024), 0) < 4, 1.0, 0.0)
    right_side = 1.0 - left_side

    def interpolate_strips(groups):
        s = [sf[d] for d in range(3)]
        t = [pltpu.roll(v, 4, 0) for v in s]
        low = sub < 4
        halo = [jnp.where(cell < 4, s[d], t[d]) for d in range(3)]
        for group in groups:
            if group == 0:
                a, b = jnp.where(low, s[0], t[1]), s[2]
            elif group == 1:
                a, b = jnp.where(low, halo[0], pltpu.roll(halo[1], 4, 0)), halo[2]
            else:
                a, b = jnp.where(low, t[0], s[1]), t[2]
            rows = stacked(jnp.concatenate([a, jnp.where(low, b, 0.0)], axis=0))
            r = dot(jnp.concatenate([rows, rows], axis=1), ws[:, 1024 * group : 1024 * group + 1024])
            w = wx[group]
            first, second = (r[0:8] + r[16:24]) * w, (r[8:16] + r[24:32]) * w
            urow[group, 0:1, :] = jnp.sum(first * left_side, axis=0, keepdims=True)
            urow[group, 1:2, :] = jnp.sum(first * right_side, axis=0, keepdims=True)
            urow[group, 2:3, :] = jnp.sum(second, axis=0, keepdims=True)

    def interpolate_tile():
        for q in range(4):
            cols = slice(256 * q, 256 * q + 256)
            a = dot(lf[...], wm[0:256, cols])
            b = dot(lf[0:192], wm[256:512, cols])
            for c in range(3):
                both = (a[64 * c : 64 * c + 64] + a[192 + 64 * c : 256 + 64 * c]) + b[64 * c : 64 * c + 64]
                part = jnp.sum(both * plane[:, cols], axis=0, keepdims=True)
                urow[1, c : c + 1, cols] = urow[1, c : c + 1, cols] + part

    def forces():
        return [brow[group] - feedback_gain * urow[group] for group in range(3)]

    def spread_strips(force):
        parts = []
        for group in (0, 2):
            f = [jnp.broadcast_to(force[group][c : c + 1], (8, 1024)) for c in range(3)]
            w = wx[group]
            v = jnp.concatenate([jnp.where(left_side > 0.5, f[0], f[1]) * w, f[2] * (w * left_side)], axis=0)
            r = dot_t(stacked(v), ws[:, 1024 * group : 1024 * group + 1024])
            r = (r[0:16, 0:128] + r[0:16, 128:256]) + r[16:32, 0:128]
            parts.append((r[0:8], r[8:16]))
        (la, lb), (ra, rb) = parts
        low = sub < 4
        mine = pack(gf, 3)
        return [
            mine[0] + jnp.where(low, la, pltpu.roll(ra, 4, 0)),
            mine[1] + jnp.where(low, pltpu.roll(la, 4, 0), ra),
            mine[2] + jnp.where(low, lb, pltpu.roll(rb, 4, 0)),
        ]

    def spread_tile(force):
        for q in range(8):
            cols = slice(128 * q, 128 * q + 128)
            for c in range(3):
                hi, lo = split(force[1][c : c + 1, cols] * plane[:, cols])
                vst[64 * c : 64 * c + 64, cols] = hi
                vst[192 + 64 * c : 256 + 64 * c, cols] = lo
        total = dot_t(vst[...], wm[0:256])
        total = (total[0:192] + total[192:384]) + dot_t(vst[0:192], wm[256:512])
        a, b = total[:, 0:128].reshape(24, 8, 128), total[:, 128:256].reshape(24, 8, 128)
        low = (sub < 4)[None]
        even = jnp.where(low, a, pltpu.roll(b, 4, 1)).reshape(24, 1, 8, 128)
        odd = jnp.where(low, pltpu.roll(a, 4, 1), b).reshape(24, 1, 8, 128)
        gf[...] = jnp.concatenate([even, odd], axis=1).reshape(3, 16, 8, 128)

    def collide_tile(step):
        def body(q, carry):
            to_east, to_west = [None] * 5, [None] * 5
            for zz in range(4):
                z = 4 * q + zz
                f = [fm[entry, z] for entry in range(19)]
                force = []
                for d in range(3):
                    force.append(jnp.where(edge4, pltpu.roll(gs[d], 124 - 8 * z, 1), gf[d, z]))
                post = collide(f, mo[0, z], [mo[1, z], mo[2, z], mo[3, z]], force)
                for entry in range(19):
                    pm[entry, z] = post[entry]
                for k in range(5):
                    a = pltpu.roll(post[EAST[k]], 5 + zz, 0) if zz < 3 else post[EAST[k]]
                    b = pltpu.roll(post[WEST[k]], zz, 0) if zz else post[WEST[k]]
                    to_east[k] = jnp.where(xs == zz, a, to_east[k]) if zz else a
                    to_west[k] = jnp.where(xs == zz, b, to_west[k]) if zz else b
            for k in range(5):
                xsp[step, q, k] = to_east[k]
                xsm[step, q, k] = to_west[k]
            row_copy(step, 0, q).start()
            row_copy(step, 1, q).start()
            return carry
        lax.fori_loop(0, 4, body, 0)

    def row_copy(step, way, q):
        src, dst, target = ((xsp, xrp, (east, me_y)), (xsm, xrm, (west, me_y)))[way]
        k = 18 + 8 * step + 4 * way + q
        return pltpu.make_async_remote_copy(
            src_ref=src.at[step, q], dst_ref=dst.at[step, q], send_sem=k_s.at[k], recv_sem=k_r.at[k],
            device_id=target, device_id_type=MESH)

    def stream_strips(strip, ext_east, ext_west):
        result = {}
        for entry in strip["want"]:
            cx, cy, cz = velocity_set[entry]
            v = strip[entry]
            if cx == 1:
                v = jnp.where(xs == 0, ext_east[entry], pltpu.roll(v, 1, 0))
            elif cx == -1:
                v = jnp.where(xs == 3, ext_west[entry], pltpu.roll(v, 7, 0))
            turn = (8 * cz + cy) % 128
            if turn:
                v = pltpu.roll(v, turn, 1)
            if cz == 1:
                v = jnp.where(zl == 0, strip[opposite(entry)], v)
            elif cz == -1:
                v = jnp.where(zl == 15, strip[opposite(entry)], v)
            result[entry] = v
        return result

    def stream_at(entry, z, step):
        cx, cy, cz = velocity_set[entry]
        zs = jnp.maximum(z - 1, 0) if cz == 1 else jnp.minimum(z + 1, 15) if cz == -1 else z
        v = pm[entry, zs]
        if cx:
            zz = zs & 3
            if cx == 1:
                row = pltpu.roll(xrp[step, zs >> 2, EAST.index(entry)], (8 - zz) & 7, 0)
                v = jnp.where(xs == 0, row, pltpu.roll(v, 1, 0))
            else:
                row = pltpu.roll(xrm[step, zs >> 2, WEST.index(entry)], 3 - zz, 0)
                v = jnp.where(xs == 3, row, pltpu.roll(v, 7, 0))
        if cy:
            r = pltpu.roll(v, 1 if cy == 1 else 127, 1)
            v = jnp.where(lane == (0 if cy == 1 else 127), pltpu.roll(r, 4, 0), r)
        if cz:
            v = jnp.where(z == (0 if cz == 1 else 15), pm[opposite(entry), z], v)
        return v

    def overlay(entry, z, v):
        strip = pltpu.roll(st[entry], 124 - 8 * z, 1)
        return jnp.where(edge1[0] if velocity_set[entry][1] == 1 else edge1[1], strip, v)

    for copy in flows:
        copy.wait()
    sf[...] = merge(p_flow[...], fl_l[...], fl_r[...])
    interpolate_strips((0, 1, 2))
    interpolate_tile()
    force = forces()
    spread_tile(force)
    strip_force = spread_strips(force)
    for d in range(3):
        gs[d] = strip_force[d]
    f = [st[entry] for entry in range(19)]
    rho, flux = moments(f)
    post = collide(f, rho, flux, strip_force)
    low = sub < 4
    for k in range(10):
        a, b = post[STRIP[2 * k]], post[STRIP[2 * k + 1]]
        p1[2 * k], p1[2 * k + 1] = a, b
        pn[k] = jnp.where(low, pltpu.roll(a, 4, 0), b)
        ps[k] = jnp.where(low, a, pltpu.roll(b, 4, 0))
    ahead_e = [pltpu.roll(post[EAST[k]], (5 + k) % 8, 0) if k != 3 else post[EAST[k]] for k in range(4)]
    ahead_w = [pltpu.roll(post[WEST[k]], k, 0) if k else post[WEST[k]] for k in range(4)]
    for k in range(1, 4):
        ahead_e[0] = jnp.where(xs == k, ahead_e[k], ahead_e[0])
        ahead_w[0] = jnp.where(xs == k, ahead_w[k], ahead_w[0])
    pe[0], pe[1] = ahead_e[0], pltpu.roll(post[EAST[4]], 5, 0)
    pw[0], pw[1] = ahead_w[0], post[WEST[4]]
    strips = [
        remote(pn, r1l, 2, (me_x, north)),
        remote(ps, r1r, 3, (me_x, south)),
        remote(pe, daa, 6, (east, north)),
        remote(pe, dab, 7, (east, south)),
        remote(pw, dba, 8, (west, north)),
        remote(pw, dbb, 9, (west, south)),
        remote(pe, gxa, 4, (east, me_y)),
        remote(pw, gxb, 5, (west, me_y)),
    ]
    collide_tile(0)
    rows = [row_copy(0, way, q) for way in range(2) for q in range(4)]

    def straight(i, carry):
        for z in range(4):
            for entry in STRAIGHT:
                fm[entry, 4 * i + z] = stream_at(entry, 4 * i + z, 0)
        return carry

    def slanted(i, carry):
        for z in range(4):
            for entry in SLANTED:
                fm[entry, 4 * i + z] = stream_at(entry, 4 * i + z, 0)
        return carry

    lax.fori_loop(0, 4, straight, 0)
    for copy in rows:
        copy.wait()
    lax.fori_loop(0, 4, slanted, 0)

    for copy in strips:
        copy.wait()
    beside_w = merge(gxa[...], daa[...], dab[...])
    beside_e = merge(gxb[...], dba[...], dbb[...])
    strip = {"want": range(19)}
    for k, entry in enumerate(STRIP):
        from_l, from_r = r1l[k // 2], r1r[k // 2]
        if k % 2:
            from_l = pltpu.roll(from_l, 4, 0)
        else:
            from_r = pltpu.roll(from_r, 4, 0)
        strip[entry] = jnp.where(own, p1[k], jnp.where(low, from_l, from_r))
    moved = stream_strips(
        strip,
        {e: pltpu.roll(beside_w[k // 4], (8 - k % 4) % 8, 0) if k % 4 else beside_w[k // 4] for k, e in enumerate(EAST)},
        {e: pltpu.roll(beside_e[k // 4], 3 - k % 4, 0) if k % 4 < 3 else beside_e[k // 4] for k, e in enumerate(WEST)})
    for entry in range(19):
        st[entry] = moved[entry]
    f = [moved[entry] for entry in range(19)]
    strip_rho, strip_flux = moments(f)
    inv = 1.0 / strip_rho
    for d in range(3):
        sf[d] = strip_flux[d] * inv
    def second(i, carry):
        for zz in range(2):
            z = 2 * i + zz
            f = [fm[entry, z] for entry in range(19)]
            for entry in EDGED:
                f[entry] = overlay(entry, z, f[entry])
                fm[entry, z] = f[entry]
            rho, flux = moments(f)
            mo[0, z] = rho
            inv = 1.0 / rho
            for d in range(3):
                mo[1 + d, z] = flux[d]
                fl[d, z] = flux[d] * inv
        return carry

    lax.fori_loop(0, 8, second, 0)
    rows_of_flow()

    interpolate_strips((1,))
    interpolate_tile()

    us[...] = jnp.zeros((128, 384), F32)
    for s in range(8):
        for c in range(3):
            us[8 + s : 9 + s, 128 * c : 128 * c + 128] = urow[1, c : c + 1, 128 * s : 128 * s + 128]
    home = sel_t[0:64].astype(BF16)
    homeward = dot_select(home, us[...])
    for c in range(3):
        back = homeward[:, 128 * c : 128 * c + 128]
        for f in range(2):
            for i in range(2):
                at = (2 * f + i) * 16
                u_ret[:, 2 * c + f, i * 128 : (i + 1) * 128] = back[at : at + 16]
    u_recv[me_y] = u_ret[me_y]
    returns = []
    for d in range(1, ny):
        peer = lax.rem(me_y + d, ny)
        copy = pltpu.make_async_remote_copy(
            src_ref=u_ret.at[peer], dst_ref=u_recv.at[me_y], send_sem=u_s.at[d], recv_sem=u_r.at[d],
            device_id=(me_x, peer), device_id_type=MESH)
        copy.start()
        returns.append(copy)

    interpolate_strips((0, 2))
    force = forces()
    spread_tile(force)
    strip_force = spread_strips(force)
    for d in range(3):
        gs[d] = strip_force[d]
    f = [st[entry] for entry in range(19)]
    post = collide(f, strip_rho, strip_flux, strip_force)
    for k, entry in enumerate(STRIP):
        p2[k] = post[entry]
    strips = [
        remote(p2.at[4:9], r2l, 12, (me_x, north)),
        remote(p2.at[12:17], r2r, 13, (me_x, south)),
        remote(p2.at[4:5], d2aa, 14, (east, north)),
        remote(p2.at[0:1], d2ab, 15, (east, south)),
        remote(p2.at[8:9], d2ba, 16, (west, north)),
        remote(p2.at[12:13], d2bb, 17, (west, south)),
    ]
    collide_tile(1)
    rows = [row_copy(1, way, q) for way in range(2) for q in range(4)]

    def leave(i, entries):
        for zz in range(4):
            for entry in entries:
                v = stream_at(entry, 4 * i + zz, 1)
                out_pop[entry, 4 * i + zz] = (v - lattice_weight[entry]) * (1.0 / deviation_unit)

    def last_straight(i, carry):
        leave(i, STRAIGHT)
        return carry

    def last_slanted(i, carry):
        leave(i, SLANTED)
        return carry

    lax.fori_loop(0, 4, last_straight, 0)
    for copy in rows:
        copy.wait()
    lax.fori_loop(0, 4, last_slanted, 0)

    for copy in strips:
        copy.wait()
    own_strip = {entry: p2[AT[entry]] for entry in range(19)}
    for k, entry in enumerate(STRIP[4:9]):
        own_strip[entry] = jnp.where(own, p2[AT[entry]], pltpu.roll(r2l[k], 4, 0))
    south_side = dict(own_strip)
    for k, entry in enumerate(STRIP[12:17]):
        south_side[entry] = jnp.where(own, p2[AT[entry]], pltpu.roll(r2r[k], 4, 0))
    south_side["want"] = STRIP[4:9] + STRIP[12:17]
    for k, entry in enumerate(STRIP[4:9]):
        south_side[entry] = own_strip[entry]
    moved = stream_strips(
        south_side,
        {7: pltpu.roll(d2aa[0], 1, 0), 9: pltpu.roll(d2ab[0], 1, 0)},
        {10: pltpu.roll(d2ba[0], 7, 0), 8: pltpu.roll(d2bb[0], 7, 0)})
    for entry in south_side["want"]:
        st[entry] = (moved[entry] - lattice_weight[entry]) * (1.0 / deviation_unit)

    def last_edges(i, carry):
        for zz in range(4):
            for entry in EDGED:
                out_pop[entry, 4 * i + zz] = overlay(entry, 4 * i + zz, out_pop[entry, 4 * i + zz])
        return carry

    lax.fori_loop(0, 4, last_edges, 0)

    for copy in returns:
        copy.wait()
    total = u_recv[0]
    for j in range(1, ny):
        total = total + u_recv[j]
    total = total / deviation_unit
    for c in range(3):
        for f in range(2):
            out_vel[c, f : f + 1, :] = total[2 * c + f : 2 * c + f + 1, :]


def per_device(nx, ny, populations, fraction, spans, stiffness):
    pop = populations.reshape(19, 16, 4, 2, 128).transpose(0, 1, 3, 2, 4).reshape(19, 16, 8, 128)
    anywhere = pl.BlockSpec(memory_space=pl.ANY)
    V = lambda *shape: pltpu.VMEM(shape, F32)
    B = lambda *shape: pltpu.VMEM(shape, BF16)
    dma = pltpu.SemaphoreType.DMA
    tile = V(19, 16, 8, 128)
    scratch = [
        V(3, 2, 256), pltpu.VMEM((2, 32), jnp.int32), pltpu.SMEM((2,), jnp.int32), V(3, 2, 256),
        tile, V(4, 16, 8, 128), V(3, 16, 8, 128), B(384, 256), V(3, 16, 8, 128), tile,
        V(6, 256), V(ny, 6, 256), V(128, 768), V(128, 128), V(3, 3, 32, 128), V(3, 32, 128),
        B(512, 1024), V(64, 1024), B(256, 3072), V(3, 8, 1024), V(3, 16, 128),
        V(3, 8, 1024), V(3, 8, 1024), B(384, 1024), V(128, 384), V(ny, 6, 256), V(ny, 6, 256),
        V(3, 8, 128), V(3, 8, 128), V(3, 8, 128), V(3, 8, 128), V(19, 8, 128),
        V(20, 8, 128), V(10, 8, 128), V(10, 8, 128), V(2, 8, 128), V(2, 8, 128), V(10, 8, 128), V(10, 8, 128),
        V(2, 8, 128), V(2, 8, 128), V(2, 8, 128), V(2, 8, 128), V(2, 8, 128), V(2, 8, 128),
        V(20, 8, 128), V(5, 8, 128), V(5, 8, 128), V(1, 8, 128), V(1, 8, 128), V(1, 8, 128), V(1, 8, 128),
        V(2, 4, 5, 8, 128), V(2, 4, 5, 8, 128), V(2, 4, 5, 8, 128), V(2, 4, 5, 8, 128), V(3, 8, 128),
        dma((ny,)), dma((ny,)), dma((ny,)), dma((ny,)), dma((34,)), dma((34,)), dma((7,)), dma((5,)),
    ]
    out, vel = pl.pallas_call(
        functools.partial(kernel, nx, ny),
        out_shape=(jax.ShapeDtypeStruct((19, 16, 8, 128), F32), jax.ShapeDtypeStruct((3, 2, 256), F32)),
        in_specs=[pl.BlockSpec(memory_space=pltpu.HBM)] * 4,
        out_specs=(pl.BlockSpec(memory_space=pltpu.VMEM),) * 2,
        scratch_shapes=scratch,
        name="lattice",
        compiler_params=pltpu.CompilerParams(
            collective_id=0, has_side_effects=True, vmem_limit_bytes=40 << 20),
    )(*[pltpu.with_memory_space_constraint(x, pltpu.HBM) for x in (
        pop, fraction.transpose(1, 0, 2), spans.reshape(spans.shape[0], spans.shape[1]), stiffness)])
    out = out.reshape(19, 16, 2, 4, 128).transpose(0, 1, 3, 2, 4).reshape(19, 16, 4, 256)
    return out, vel.transpose(1, 0, 2)


def solution(mesh):
    placed = (P(None, None, "gx", "gy"), P("gx", None, "gy"), P("gx", None, None), P("gx"))
    return jax.shard_map(
        functools.partial(per_device, mesh.shape["gx"], mesh.shape["gy"]),
        mesh=mesh,
        in_specs=placed,
        out_specs=(P(None, None, "gx", "gy"), P("gx", None, "gy")),
        check_vma=False,
    )
```

```python
import functools
import math

import jax
import jax.numpy as jnp
from jax import lax
from jax.experimental import pallas as pl
from jax.experimental.pallas import tpu as pltpu
from jax.sharding import PartitionSpec as P

F32 = jnp.float32
BF16 = jnp.bfloat16
MESH = pl.DeviceIdType.MESH

velocity_set = (
    (0, 0, 0), (1, 0, 0), (-1, 0, 0), (0, 1, 0), (0, -1, 0), (0, 0, 1), (0, 0, -1),
    (1, 1, 0), (-1, -1, 0), (1, -1, 0), (-1, 1, 0), (1, 0, 1), (-1, 0, -1),
    (1, 0, -1), (-1, 0, 1), (0, 1, 1), (0, -1, -1), (0, 1, -1), (0, -1, 1),
)
lattice_weight = (1.0 / 3.0,) + (1.0 / 18.0,) * 6 + (1.0 / 36.0,) * 12
relax_time = 0.8
deviation_unit = 0.002
feedback_gain = 2.0
stiff_unit = 0.002

STRIP = (9, 1, 11, 13, 7, 3, 15, 17, 10, 2, 12, 14, 8, 4, 16, 18, 9, 0, 5, 6)
AT = {entry: STRIP.index(entry) for entry in range(19)}
EAST, WEST = STRIP[0:5], STRIP[8:13]
STRAIGHT = tuple(e for e in range(19) if velocity_set[e][0] == 0)
SLANTED = EAST + WEST
EDGED = tuple(e for e in range(19) if velocity_set[e][1] != 0)
PAIRS = tuple((i, i + 1) for i in range(1, 19, 2))


def opposite(entry):
    return entry + 1 if entry % 2 == 1 else entry - 1


def moments(f):
    rho = f[0]
    for entry in range(1, 19):
        rho = rho + f[entry]
    flux = []
    for dim in range(3):
        total = None
        for a, b in PAIRS:
            c = velocity_set[a][dim]
            if c:
                term = f[a] - f[b] if c > 0 else f[b] - f[a]
                total = term if total is None else total + term
        flux.append(total)
    return rho, flux


def project(vector, parts):
    total = None
    for dim in range(3):
        if vector[dim]:
            if total is None:
                total = parts[dim] if vector[dim] > 0 else -parts[dim]
            else:
                total = total + parts[dim] if vector[dim] > 0 else total - parts[dim]
    return total


def collide(f, rho, flux, force):
    factor = 1.0 - 0.5 / relax_time
    keep, gain = 1.0 - 1.0 / relax_time, 1.0 / relax_time
    mom = [flux[d] + 0.5 * force[d] for d in range(3)]
    inv = 1.0 / rho
    u = [mom[d] * inv for d in range(3)]
    usq = u[0] * mom[0] + u[1] * mom[1] + u[2] * mom[2]
    ug = u[0] * force[0] + u[1] * force[1] + u[2] * force[2]
    base = gain * (rho - 1.5 * usq) - (3.0 * factor) * ug
    post = [None] * 19
    post[0] = keep * f[0] + lattice_weight[0] * base
    for a, b in PAIRS:
        vector = velocity_set[a]
        cu, cm, cg = project(vector, u), project(vector, mom), project(vector, force)
        even = base + cu * ((4.5 * gain) * cm + (9.0 * factor) * cg)
        odd = (3.0 * gain) * cm + (3.0 * factor) * cg
        w = lattice_weight[a]
        post[a] = keep * f[a] + w * (even + odd)
        post[b] = keep * f[b] + w * (even - odd)
    return post


def split(a):
    hi = a.astype(BF16)
    return hi, (a - hi.astype(F32)).astype(BF16)


def dot(a, b):
    return jnp.dot(a, b, preferred_element_type=F32)


def dot_t(a, b):
    return lax.dot_general(a, b, (((1,), (1,)), ((), ())), preferred_element_type=F32)


def stacked(a):
    return jnp.concatenate(split(a), axis=0)


def dot_select(pick, b):
    h = b.astype(BF16)
    rest = b - h.astype(F32)
    m = rest.astype(BF16)
    l = (rest - m.astype(F32)).astype(BF16)
    return (dot(pick, h) + dot(pick, m)) + dot(pick, l)


def pattern(n):
    m = n & 3
    one, zero = jnp.float32(1.0), jnp.float32(0.0)
    c = jnp.where(m == 0, one, jnp.where(m == 2, -one, zero))
    s = jnp.where(m == 1, one, jnp.where(m == 3, -one, zero))
    return n.astype(F32), c, s


def weight(row, pat):
    x, c, s = row
    n, cp, sp = pat
    return jnp.where(jnp.abs(x - n) < 2.0, 0.25 + 0.25 * (c * cp + s * sp), 0.0)


def iota(shape, dim):
    return lax.broadcasted_iota(jnp.int32, shape, dim)


def kernel(nx, ny, pop_in, frac_in, spans_in, stiff_in, out_pop, out_vel,
           frac, spans, stiff, vel,
           fm, mo, fl, lf, gf, pm, fr_send, fr_all, data, sel_t, xyz, bend, wm, plane,
           ws, wx, wz_rows, brow, urow, vst, us, u_ret, u_recv,
           p_flow, fl_l, fl_r, sf, st, p1, pn, ps, pe, pw, r1l, r1r, gxa, gxb, daa, dab, dba, dbb,
           p2, r2l, r2r, d2aa, d2ab, d2ba, d2bb, xsp, xsm, xrp, xrm, gs,
           ag_s, ag_r, u_s, u_r, k_s, k_r, in_s, out_s):
    me_x, me_y = lax.axis_index("gx"), lax.axis_index("gy")
    east, west = lax.rem(me_x + 1, nx), lax.rem(me_x + nx - 1, nx)
    north, south = lax.rem(me_y + 1, ny), lax.rem(me_y + ny - 1, ny)
    tile_y = 256

    small = [pltpu.make_async_copy(a, b, in_s.at[4 + k])
             for k, (a, b) in enumerate(((frac_in, frac), (spans_in, spans), (stiff_in, stiff)))]
    small[0].start()
    barrier = pltpu.get_barrier_semaphore()
    partners = [(me_x, lax.rem(me_y + d, ny)) for d in range(1, ny)]
    partners += [(east, me_y), (west, me_y), (east, north), (east, south), (west, north), (west, south)]
    for partner in partners:
        pl.semaphore_signal(barrier, inc=1, device_id=partner, device_id_type=MESH)

    def remote(src, dst, k, target):
        copy = pltpu.make_async_remote_copy(
            src_ref=src, dst_ref=dst, send_sem=k_s.at[k], recv_sem=k_r.at[k],
            device_id=target, device_id_type=MESH)
        copy.start()
        return copy

    lane, sub = iota((8, 128), 1), iota((8, 128), 0)
    cell, zl, xs = lane & 7, lane >> 3, sub & 3
    own = (sub >> 2) + (cell >> 2) == 1
    edge1 = ((sub < 4) & (lane == 0), (sub >= 4) & (lane == 127))
    edge4 = (lane >> 2) + (sub >> 2) * 32 == 0
    edge4 = edge4 | ((sub >= 4) & (lane >= 124))

    small[1].start()
    small[2].start()
    loads = []
    for q in range(4):
        part = pl.ds(4 * q, 4)
        loads.append(pltpu.make_async_copy(pop_in.at[:, part], fm.at[:, part], in_s.at[q]))
        loads[q].start()
    small[0].wait()
    for c in range(3):
        for f in range(2):
            fr_send[2 * c + f : 2 * c + f + 1, :] = frac[c, f : f + 1, :]
    fr_all[me_y] = fr_send[...]
    pl.semaphore_wait(barrier, len(partners))
    gathers = []
    for d in range(1, ny):
        copy = pltpu.make_async_remote_copy(
            src_ref=fr_send, dst_ref=fr_all.at[me_y], send_sem=ag_s.at[d], recv_sem=ag_r.at[d],
            device_id=(me_x, lax.rem(me_y + d, ny)), device_id_type=MESH)
        copy.start()
        gathers.append(copy)

    def first(z, carry):
        f = []
        for entry in range(19):
            f.append(lattice_weight[entry] + deviation_unit * fm[entry, z])
            fm[entry, z] = f[entry]
        rho, flux = moments(f)
        mo[0, z] = rho
        inv = 1.0 / rho
        for d in range(3):
            mo[1 + d, z] = flux[d]
            fl[d, z] = flux[d] * inv
        return carry

    for q in range(4):
        loads[q].wait()
        lax.fori_loop(4 * q, 4 * q + 4, first, 0)

    def pack(ref, n):
        def body(z, acc):
            rolled = pltpu.roll(ref[:, z], 8 * z + 4, 2)
            return jnp.where(zl[None] == z, rolled, acc)
        return lax.fori_loop(0, 16, body, jnp.zeros((n, 8, 128), F32))

    p_flow[...] = pack(fl, 3)
    flows = [remote(p_flow, fl_l, 0, (me_x, north)), remote(p_flow, fl_r, 1, (me_x, south))]
    small[1].wait()
    small[2].wait()

    st[...] = pack(fm, 19)

    def rows_of_flow():
        v = fl[...].reshape(3, 8, 2, 8, 128)
        a, b = v[:, :, 0].reshape(24, 8, 128), v[:, :, 1].reshape(24, 8, 128)
        low = (sub < 4)[None]
        halves = (jnp.where(low, a, pltpu.roll(b, 4, 1)), jnp.where(low, pltpu.roll(a, 4, 1), b))
        for k, half in enumerate(halves):
            hi, lo = split(half.reshape(192, 128))
            lf[0:192, 128 * k : 128 * k + 128] = hi
            lf[192:384, 128 * k : 128 * k + 128] = lo

    rows_of_flow()

    span_cols = []
    row16, lane32 = iota((16, 32), 0), iota((16, 32), 1)
    for f in range(2):
        line = jnp.broadcast_to(spans[f : f + 1, :].astype(F32), (16, 32))
        for i in range(2):
            span_cols.append(jnp.sum(jnp.where(lane32 == 2 * row16 + i, line, 0.0), axis=1, keepdims=True))
    span_col = jnp.concatenate(span_cols + [jnp.full((64, 1), -1.0, F32)], axis=0)
    r128, l128 = iota((128, 128), 0), iota((128, 128), 1)
    target = me_y + (l128 >> 3) - 1
    target = jnp.where(target < 0, target + ny, jnp.where(target >= ny, target - ny, target)).astype(F32)
    match = jnp.where((jnp.broadcast_to(span_col, (128, 128)) == target) & (l128 < 24), 1.0, 0.0)
    before = jnp.where(l128 < r128, 1.0, 0.0).astype(BF16)
    rank = jnp.dot(before, match.astype(BF16), preferred_element_type=F32)
    chosen = jnp.where(rank == (l128 & 7).astype(F32), match, 0.0)
    sel_t[...] = chosen
    sel = chosen.T
    valid = jnp.sum(sel, axis=1, keepdims=True)[0:32]
    pick = sel[0:32].astype(BF16)

    for copy in gathers:
        copy.wait_recv()
    anchor = (me_x * 4).astype(F32)
    l16, r16 = iota((16, 128), 1), iota((16, 128), 0)
    data[64:128, :] = jnp.zeros((64, 768), F32)
    for f in range(2):
        strength = stiff[f].astype(F32) * (stiff_unit / tile_y)
        for c in range(3):
            x = []
            for i in range(2):
                part = fr_all[:, 2 * c + f, i * 128 : (i + 1) * 128]
                if c == 0:
                    x.append((anchor + 1.0) + part * (4 - 3.01))
                elif c == 1:
                    x.append(span_cols[2 * f + i] * tile_y + part * tile_y)
                else:
                    x.append(1.0 + part * (16 - 3.01))
            ahead = [pltpu.roll(x[i], 127, 1) for i in range(2)]
            g0 = jnp.where(l16 == 127, ahead[1], ahead[0]) - x[0]
            g1 = jnp.where(l16 == 127, pltpu.roll(ahead[0], 15, 0), ahead[1]) - x[1]
            if c == 1:
                period = float(ny * tile_y)
                half = 0.5 * period
                g0 = jnp.where(g0 > half, g0 - period, jnp.where(g0 < -half, g0 + period, g0))
                g1 = jnp.where(g1 > half, g1 - period, jnp.where(g1 < -half, g1 + period, g1))
            g1 = jnp.where((l16 == 127) & (r16 == 15), 0.0, g1)
            b0, b1 = pltpu.roll(g0, 1, 1), pltpu.roll(g1, 1, 1)
            prev0 = jnp.where(l16 == 0, pltpu.roll(b1, 1, 0), b0)
            prev1 = jnp.where(l16 == 0, b0, b1)
            at = f * 32
            cols, more = slice(128 * c, 128 * c + 128), slice(384 + 128 * c, 512 + 128 * c)
            data[at : at + 16, cols] = x[0]
            data[at + 16 : at + 32, cols] = x[1]
            data[at : at + 16, more] = (g0 - prev0) * strength
            data[at + 16 : at + 32, more] = (g1 - prev1) * strength
    slots_of = dot_select(pick, data[...])
    for c in range(3):
        bend[c] = slots_of[:, 384 + 128 * c : 512 + 128 * c]
        x = slots_of[:, 128 * c : 128 * c + 128]
        if c == 0:
            x = x - anchor
        elif c == 1:
            x = x - (me_y * tile_y).astype(F32)
            period = float(ny * tile_y)
            x = jnp.where(x > 0.5 * period, x - period, jnp.where(x < -0.5 * period, x + period, x))
            x = jnp.where(valid > 0.5, x, 1.0e6)
        base = jnp.floor(x)
        part = (0.5 * math.pi) * (x - base)
        cos, sin = jnp.cos(part), jnp.sin(part)
        turn = base - 4.0 * jnp.floor(0.25 * base)
        xyz[c, 0] = x
        xyz[c, 1] = jnp.where(turn == 0.0, cos, jnp.where(turn == 1.0, -sin, jnp.where(turn == 2.0, -cos, sin)))
        xyz[c, 2] = jnp.where(turn == 0.0, sin, jnp.where(turn == 1.0, cos, jnp.where(turn == 2.0, -sin, -cos)))

    pat_z = pattern(iota((16, 128), 0))
    pat_low, pat_high = pattern(sub - 4), pattern(sub + (tile_y - 4))
    pat_own = pattern(jnp.where(sub < 4, sub - 4, sub + (tile_y - 4)))
    pat_x, pat_y = pattern(xs), pattern(sub)
    down = iota((16, 128), 0).astype(F32)

    def weights(s, carry):
        def line(group, c):
            return [xyz[c, k, pl.ds(group * 8 + s, 1), :] for k in range(3)]
        where_s = pl.ds(pl.multiple_of(s * 128, 128), 128)

        for group in range(3):
            lx, ly, lz = line(group, 0), line(group, 1), line(group, 2)
            across = weight(lx, pat_x)
            wx[group, :, where_s] = across
            wz_rows[group] = weight(lz, pat_z)
            wz = [jnp.broadcast_to(wz_rows[group, z : z + 1, :], (8, 128)) for z in range(16)]
            columns = pl.ds(pl.multiple_of(group * 1024 + s * 128, 128), 128)
            wy = weight(ly, (pat_low, pat_own, pat_high)[group])
            for z in range(0, 16, 2):
                hi, lo = split(jnp.concatenate([wz[z] * wy, wz[z + 1] * wy], axis=0))
                ws[8 * z : 8 * z + 16, columns] = hi
                ws[128 + 8 * z : 144 + 8 * z, columns] = lo
            if group == 1:
                tall = 0.25 + 0.25 * (ly[1] * pat_y[1] + ly[2] * pat_y[2])
                hi8 = tall.astype(BF16).astype(F32)
                hi, lo = jnp.concatenate([hi8, hi8], axis=0), jnp.concatenate([tall - hi8, tall - hi8], axis=0)
                gap = ly[0] - down
                for r in range(16):
                    near = jnp.abs(gap - 16.0 * r) < 2.0
                    wm[16 * r : 16 * r + 16, where_s] = jnp.where(near, hi, 0.0).astype(BF16)
                    wm[256 + 16 * r : 272 + 16 * r, where_s] = jnp.where(near, lo, 0.0).astype(BF16)
                for i in range(8):
                    plane[8 * i : 8 * i + 8, where_s] = jnp.where(sub < 4, wz[2 * i], wz[2 * i + 1]) * across
            for c in range(3):
                brow[group, c : c + 1, where_s] = bend[c, pl.ds(group * 8 + s, 1), :]
        return carry

    lax.fori_loop(0, 8, weights, 0)
    for group in range(3):
        brow[group, 3:8, :] = jnp.zeros((5, 1024), F32)

    def merge(centre, left, right):
        n = centre.shape[0]
        side = jnp.where((cell < 4)[None], left, right)
        return jnp.where(own[None], centre, pltpu.roll(side, 4, 1))

    left_side = jnp.where(iota((8, 1024), 0) < 4, 1.0, 0.0)
    right_side = 1.0 - left_side

    def interpolate_strips(groups):
        s = [sf[d] for d in range(3)]
        t = [pltpu.roll(v, 4, 0) for v in s]
        low = sub < 4
        halo = [jnp.where(cell < 4, s[d], t[d]) for d in range(3)]
        for group in groups:
            if group == 0:
                a, b = jnp.where(low, s[0], t[1]), s[2]
            elif group == 1:
                a, b = jnp.where(low, halo[0], pltpu.roll(halo[1], 4, 0)), halo[2]
            else:
                a, b = jnp.where(low, t[0], s[1]), t[2]
            rows = stacked(jnp.concatenate([a, jnp.where(low, b, 0.0)], axis=0))
            r = dot(jnp.concatenate([rows, rows], axis=1), ws[:, 1024 * group : 1024 * group + 1024])
            w = wx[group]
            first, second = (r[0:8] + r[16:24]) * w, (r[8:16] + r[24:32]) * w
            urow[group, 0:1, :] = jnp.sum(first * left_side, axis=0, keepdims=True)
            urow[group, 1:2, :] = jnp.sum(first * right_side, axis=0, keepdims=True)
            urow[group, 2:3, :] = jnp.sum(second, axis=0, keepdims=True)

    def interpolate_tile():
        for q in range(4):
            cols = slice(256 * q, 256 * q + 256)
            a = dot(lf[...], wm[0:256, cols])
            b = dot(lf[0:192], wm[256:512, cols])
            for c in range(3):
                both = (a[64 * c : 64 * c + 64] + a[192 + 64 * c : 256 + 64 * c]) + b[64 * c : 64 * c + 64]
                part = jnp.sum(both * plane[:, cols], axis=0, keepdims=True)
                urow[1, c : c + 1, cols] = urow[1, c : c + 1, cols] + part

    def forces():
        return [brow[group] - feedback_gain * urow[group] for group in range(3)]

    def spread_strips(force):
        parts = []
        for group in (0, 2):
            f = [jnp.broadcast_to(force[group][c : c + 1], (8, 1024)) for c in range(3)]
            w = wx[group]
            v = jnp.concatenate([jnp.where(left_side > 0.5, f[0], f[1]) * w, f[2] * (w * left_side)], axis=0)
            r = dot_t(stacked(v), ws[:, 1024 * group : 1024 * group + 1024])
            r = (r[0:16, 0:128] + r[0:16, 128:256]) + r[16:32, 0:128]
            parts.append((r[0:8], r[8:16]))
        (la, lb), (ra, rb) = parts
        low = sub < 4
        mine = pack(gf, 3)
        return [
            mine[0] + jnp.where(low, la, pltpu.roll(ra, 4, 0)),
            mine[1] + jnp.where(low, pltpu.roll(la, 4, 0), ra),
            mine[2] + jnp.where(low, lb, pltpu.roll(rb, 4, 0)),
        ]

    def spread_tile(force):
        for q in range(8):
            cols = slice(128 * q, 128 * q + 128)
            for c in range(3):
                hi, lo = split(force[1][c : c + 1, cols] * plane[:, cols])
                vst[64 * c : 64 * c + 64, cols] = hi
                vst[192 + 64 * c : 256 + 64 * c, cols] = lo
        total = dot_t(vst[...], wm[0:256])
        total = (total[0:192] + total[192:384]) + dot_t(vst[0:192], wm[256:512])
        a, b = total[:, 0:128].reshape(24, 8, 128), total[:, 128:256].reshape(24, 8, 128)
        low = (sub < 4)[None]
        even = jnp.where(low, a, pltpu.roll(b, 4, 1)).reshape(24, 1, 8, 128)
        odd = jnp.where(low, pltpu.roll(a, 4, 1), b).reshape(24, 1, 8, 128)
        gf[...] = jnp.concatenate([even, odd], axis=1).reshape(3, 16, 8, 128)

    def collide_tile(step):
        def body(q, carry):
            to_east, to_west = [None] * 5, [None] * 5
            for zz in range(4):
                z = 4 * q + zz
                f = [fm[entry, z] for entry in range(19)]
                force = []
                for d in range(3):
                    force.append(jnp.where(edge4, pltpu.roll(gs[d], 124 - 8 * z, 1), gf[d, z]))
                post = collide(f, mo[0, z], [mo[1, z], mo[2, z], mo[3, z]], force)
                for entry in range(19):
                    pm[entry, z] = post[entry]
                for k in range(5):
                    a = pltpu.roll(post[EAST[k]], 5 + zz, 0) if zz < 3 else post[EAST[k]]
                    b = pltpu.roll(post[WEST[k]], zz, 0) if zz else post[WEST[k]]
                    to_east[k] = jnp.where(xs == zz, a, to_east[k]) if zz else a
                    to_west[k] = jnp.where(xs == zz, b, to_west[k]) if zz else b
            for k in range(5):
                xsp[step, q, k] = to_east[k]
                xsm[step, q, k] = to_west[k]
            row_copy(step, 0, q).start()
            row_copy(step, 1, q).start()
            return carry
        lax.fori_loop(0, 4, body, 0)

    def row_copy(step, way, q):
        src, dst, target = ((xsp, xrp, (east, me_y)), (xsm, xrm, (west, me_y)))[way]
        k = 18 + 8 * step + 4 * way + q
        return pltpu.make_async_remote_copy(
            src_ref=src.at[step, q], dst_ref=dst.at[step, q], send_sem=k_s.at[k], recv_sem=k_r.at[k],
            device_id=target, device_id_type=MESH)

    def stream_strips(strip, ext_east, ext_west):
        result = {}
        for entry in strip["want"]:
            cx, cy, cz = velocity_set[entry]
            v = strip[entry]
            if cx == 1:
                v = jnp.where(xs == 0, ext_east[entry], pltpu.roll(v, 1, 0))
            elif cx == -1:
                v = jnp.where(xs == 3, ext_west[entry], pltpu.roll(v, 7, 0))
            turn = (8 * cz + cy) % 128
            if turn:
                v = pltpu.roll(v, turn, 1)
            if cz == 1:
                v = jnp.where(zl == 0, strip[opposite(entry)], v)
            elif cz == -1:
                v = jnp.where(zl == 15, strip[opposite(entry)], v)
            result[entry] = v
        return result

    def stream_at(entry, z, step):
        cx, cy, cz = velocity_set[entry]
        zs = jnp.maximum(z - 1, 0) if cz == 1 else jnp.minimum(z + 1, 15) if cz == -1 else z
        v = pm[entry, zs]
        if cx:
            zz = zs & 3
            if cx == 1:
                row = pltpu.roll(xrp[step, zs >> 2, EAST.index(entry)], (8 - zz) & 7, 0)
                v = jnp.where(xs == 0, row, pltpu.roll(v, 1, 0))
            else:
                row = pltpu.roll(xrm[step, zs >> 2, WEST.index(entry)], 3 - zz, 0)
                v = jnp.where(xs == 3, row, pltpu.roll(v, 7, 0))
        if cy:
            r = pltpu.roll(v, 1 if cy == 1 else 127, 1)
            v = jnp.where(lane == (0 if cy == 1 else 127), pltpu.roll(r, 4, 0), r)
        if cz:
            v = jnp.where(z == (0 if cz == 1 else 15), pm[opposite(entry), z], v)
        return v

    def overlay(entry, z, v):
        strip = pltpu.roll(st[entry], 124 - 8 * z, 1)
        return jnp.where(edge1[0] if velocity_set[entry][1] == 1 else edge1[1], strip, v)

    for copy in flows:
        copy.wait_recv()
    sf[...] = merge(p_flow[...], fl_l[...], fl_r[...])
    interpolate_strips((0, 1, 2))
    interpolate_tile()
    force = forces()
    spread_tile(force)
    strip_force = spread_strips(force)
    for d in range(3):
        gs[d] = strip_force[d]
    f = [st[entry] for entry in range(19)]
    rho, flux = moments(f)
    post = collide(f, rho, flux, strip_force)
    low = sub < 4
    for k in range(10):
        a, b = post[STRIP[2 * k]], post[STRIP[2 * k + 1]]
        p1[2 * k], p1[2 * k + 1] = a, b
        pn[k] = jnp.where(low, pltpu.roll(a, 4, 0), b)
        ps[k] = jnp.where(low, a, pltpu.roll(b, 4, 0))
    ahead_e = [pltpu.roll(post[EAST[k]], (5 + k) % 8, 0) if k != 3 else post[EAST[k]] for k in range(4)]
    ahead_w = [pltpu.roll(post[WEST[k]], k, 0) if k else post[WEST[k]] for k in range(4)]
    for k in range(1, 4):
        ahead_e[0] = jnp.where(xs == k, ahead_e[k], ahead_e[0])
        ahead_w[0] = jnp.where(xs == k, ahead_w[k], ahead_w[0])
    pe[0], pe[1] = ahead_e[0], pltpu.roll(post[EAST[4]], 5, 0)
    pw[0], pw[1] = ahead_w[0], post[WEST[4]]
    strips = [
        remote(pn, r1l, 2, (me_x, north)),
        remote(ps, r1r, 3, (me_x, south)),
        remote(pe, daa, 6, (east, north)),
        remote(pe, dab, 7, (east, south)),
        remote(pw, dba, 8, (west, north)),
        remote(pw, dbb, 9, (west, south)),
        remote(pe, gxa, 4, (east, me_y)),
        remote(pw, gxb, 5, (west, me_y)),
    ]
    collide_tile(0)
    rows = [row_copy(0, way, q) for way in range(2) for q in range(4)]

    def straight(i, carry):
        for z in range(4):
            for entry in STRAIGHT:
                fm[entry, 4 * i + z] = stream_at(entry, 4 * i + z, 0)
        return carry

    def slanted(i, carry):
        for z in range(4):
            for entry in SLANTED:
                fm[entry, 4 * i + z] = stream_at(entry, 4 * i + z, 0)
        return carry

    lax.fori_loop(0, 4, straight, 0)
    for copy in rows:
        copy.wait_recv()
    lax.fori_loop(0, 4, slanted, 0)

    for copy in strips:
        copy.wait_recv()
    beside_w = merge(gxa[...], daa[...], dab[...])
    beside_e = merge(gxb[...], dba[...], dbb[...])
    strip = {"want": range(19)}
    for k, entry in enumerate(STRIP):
        from_l, from_r = r1l[k // 2], r1r[k // 2]
        if k % 2:
            from_l = pltpu.roll(from_l, 4, 0)
        else:
            from_r = pltpu.roll(from_r, 4, 0)
        strip[entry] = jnp.where(own, p1[k], jnp.where(low, from_l, from_r))
    moved = stream_strips(
        strip,
        {e: pltpu.roll(beside_w[k // 4], (8 - k % 4) % 8, 0) if k % 4 else beside_w[k // 4] for k, e in enumerate(EAST)},
        {e: pltpu.roll(beside_e[k // 4], 3 - k % 4, 0) if k % 4 < 3 else beside_e[k // 4] for k, e in enumerate(WEST)})
    for entry in range(19):
        st[entry] = moved[entry]
    f = [moved[entry] for entry in range(19)]
    strip_rho, strip_flux = moments(f)
    inv = 1.0 / strip_rho
    for d in range(3):
        sf[d] = strip_flux[d] * inv
    def second(i, carry):
        for zz in range(2):
            z = 2 * i + zz
            f = [fm[entry, z] for entry in range(19)]
            for entry in EDGED:
                f[entry] = overlay(entry, z, f[entry])
                fm[entry, z] = f[entry]
            rho, flux = moments(f)
            mo[0, z] = rho
            inv = 1.0 / rho
            for d in range(3):
                mo[1 + d, z] = flux[d]
                fl[d, z] = flux[d] * inv
        return carry

    lax.fori_loop(0, 8, second, 0)
    rows_of_flow()

    sent = gathers + flows + strips + rows
    interpolate_strips((1,))
    interpolate_tile()

    us[...] = jnp.zeros((128, 384), F32)
    for s in range(8):
        for c in range(3):
            us[8 + s : 9 + s, 128 * c : 128 * c + 128] = urow[1, c : c + 1, 128 * s : 128 * s + 128]
    home = sel_t[0:64].astype(BF16)
    homeward = dot_select(home, us[...])
    for c in range(3):
        back = homeward[:, 128 * c : 128 * c + 128]
        for f in range(2):
            for i in range(2):
                at = (2 * f + i) * 16
                u_ret[:, 2 * c + f, i * 128 : (i + 1) * 128] = back[at : at + 16]
    u_recv[me_y] = u_ret[me_y]
    returns = []
    for d in range(1, ny):
        peer = lax.rem(me_y + d, ny)
        copy = pltpu.make_async_remote_copy(
            src_ref=u_ret.at[peer], dst_ref=u_recv.at[me_y], send_sem=u_s.at[d], recv_sem=u_r.at[d],
            device_id=(me_x, peer), device_id_type=MESH)
        copy.start()
        returns.append(copy)

    interpolate_strips((0, 2))
    force = forces()
    spread_tile(force)
    strip_force = spread_strips(force)
    for d in range(3):
        gs[d] = strip_force[d]
    f = [st[entry] for entry in range(19)]
    post = collide(f, strip_rho, strip_flux, strip_force)
    for k, entry in enumerate(STRIP):
        p2[k] = post[entry]
    strips = [
        remote(p2.at[4:9], r2l, 12, (me_x, north)),
        remote(p2.at[12:17], r2r, 13, (me_x, south)),
        remote(p2.at[4:5], d2aa, 14, (east, north)),
        remote(p2.at[0:1], d2ab, 15, (east, south)),
        remote(p2.at[8:9], d2ba, 16, (west, north)),
        remote(p2.at[12:13], d2bb, 17, (west, south)),
    ]
    collide_tile(1)
    rows = [row_copy(1, way, q) for way in range(2) for q in range(4)]

    def leave(i, entries):
        for zz in range(4):
            for entry in entries:
                v = stream_at(entry, 4 * i + zz, 1)
                out_pop[entry, 4 * i + zz] = (v - lattice_weight[entry]) * (1.0 / deviation_unit)

    def last_straight(i, carry):
        leave(i, STRAIGHT)
        return carry

    def last_slanted(i, carry):
        leave(i, SLANTED)
        return carry

    lax.fori_loop(0, 4, last_straight, 0)
    for copy in sent + strips + returns:
        copy.wait_send()
    for copy in rows:
        copy.wait_recv()
    lax.fori_loop(0, 4, last_slanted, 0)

    for copy in strips:
        copy.wait_recv()
    own_strip = {entry: p2[AT[entry]] for entry in range(19)}
    for k, entry in enumerate(STRIP[4:9]):
        own_strip[entry] = jnp.where(own, p2[AT[entry]], pltpu.roll(r2l[k], 4, 0))
    south_side = dict(own_strip)
    for k, entry in enumerate(STRIP[12:17]):
        south_side[entry] = jnp.where(own, p2[AT[entry]], pltpu.roll(r2r[k], 4, 0))
    south_side["want"] = STRIP[4:9] + STRIP[12:17]
    for k, entry in enumerate(STRIP[4:9]):
        south_side[entry] = own_strip[entry]
    moved = stream_strips(
        south_side,
        {7: pltpu.roll(d2aa[0], 1, 0), 9: pltpu.roll(d2ab[0], 1, 0)},
        {10: pltpu.roll(d2ba[0], 7, 0), 8: pltpu.roll(d2bb[0], 7, 0)})
    for entry in south_side["want"]:
        st[entry] = (moved[entry] - lattice_weight[entry]) * (1.0 / deviation_unit)

    def last_edges(i, carry):
        for zz in range(4):
            for entry in EDGED:
                out_pop[entry, 4 * i + zz] = overlay(entry, 4 * i + zz, out_pop[entry, 4 * i + zz])
        return carry

    lax.fori_loop(0, 4, last_edges, 0)

    for copy in rows:
        copy.wait_send()
    for copy in returns:
        copy.wait_recv()
    total = u_recv[0]
    for j in range(1, ny):
        total = total + u_recv[j]
    total = total / deviation_unit
    for c in range(3):
        for f in range(2):
            out_vel[c, f : f + 1, :] = total[2 * c + f : 2 * c + f + 1, :]


def per_device(nx, ny, populations, fraction, spans, stiffness):
    pop = populations.reshape(19, 16, 4, 2, 128).transpose(0, 1, 3, 2, 4).reshape(19, 16, 8, 128)
    anywhere = pl.BlockSpec(memory_space=pl.ANY)
    V = lambda *shape: pltpu.VMEM(shape, F32)
    B = lambda *shape: pltpu.VMEM(shape, BF16)
    dma = pltpu.SemaphoreType.DMA
    tile = V(19, 16, 8, 128)
    scratch = [
        V(3, 2, 256), pltpu.VMEM((2, 32), jnp.int32), pltpu.SMEM((2,), jnp.int32), V(3, 2, 256),
        tile, V(4, 16, 8, 128), V(3, 16, 8, 128), B(384, 256), V(3, 16, 8, 128), tile,
        V(6, 256), V(ny, 6, 256), V(128, 768), V(128, 128), V(3, 3, 32, 128), V(3, 32, 128),
        B(512, 1024), V(64, 1024), B(256, 3072), V(3, 8, 1024), V(3, 16, 128),
        V(3, 8, 1024), V(3, 8, 1024), B(384, 1024), V(128, 384), V(ny, 6, 256), V(ny, 6, 256),
        V(3, 8, 128), V(3, 8, 128), V(3, 8, 128), V(3, 8, 128), V(19, 8, 128),
        V(20, 8, 128), V(10, 8, 128), V(10, 8, 128), V(2, 8, 128), V(2, 8, 128), V(10, 8, 128), V(10, 8, 128),
        V(2, 8, 128), V(2, 8, 128), V(2, 8, 128), V(2, 8, 128), V(2, 8, 128), V(2, 8, 128),
        V(20, 8, 128), V(5, 8, 128), V(5, 8, 128), V(1, 8, 128), V(1, 8, 128), V(1, 8, 128), V(1, 8, 128),
        V(2, 4, 5, 8, 128), V(2, 4, 5, 8, 128), V(2, 4, 5, 8, 128), V(2, 4, 5, 8, 128), V(3, 8, 128),
        dma((ny,)), dma((ny,)), dma((ny,)), dma((ny,)), dma((34,)), dma((34,)), dma((7,)), dma((5,)),
    ]
    out, vel = pl.pallas_call(
        functools.partial(kernel, nx, ny),
        out_shape=(jax.ShapeDtypeStruct((19, 16, 8, 128), F32), jax.ShapeDtypeStruct((3, 2, 256), F32)),
        in_specs=[pl.BlockSpec(memory_space=pltpu.HBM)] * 4,
        out_specs=(pl.BlockSpec(memory_space=pltpu.VMEM),) * 2,
        scratch_shapes=scratch,
        name="lattice",
        compiler_params=pltpu.CompilerParams(
            collective_id=0, has_side_effects=True, vmem_limit_bytes=40 << 20),
    )(*[pltpu.with_memory_space_constraint(x, pltpu.HBM) for x in (
        pop, fraction.transpose(1, 0, 2), spans.reshape(spans.shape[0], spans.shape[1]), stiffness)])
    out = out.reshape(19, 16, 2, 4, 128).transpose(0, 1, 3, 2, 4).reshape(19, 16, 4, 256)
    return out, vel.transpose(1, 0, 2)


def solution(mesh):
    placed = (P(None, None, "gx", "gy"), P("gx", None, "gy"), P("gx", None, None), P("gx"))
    return jax.shard_map(
        functools.partial(per_device, mesh.shape["gx"], mesh.shape["gy"]),
        mesh=mesh,
        in_specs=placed,
        out_specs=(P(None, None, "gx", "gy"), P("gx", None, "gy")),
        check_vma=False,
    )
```
